512 devices in a mesh: scen: 32 (over z_hi, y, core), clus: 16 (over z_lo, x).
Axes of the slice: x: 4, y: 8, z: 8 (z_hi: 2, z_lo: 4; z = z_hi * 4 + z_lo), core: 2. Of those that a mesh axis runs over, the one named last changes fastest.
Arguments:
- factors: bfloat16 [512, 64, 36864], P('scen', 'clus'), may hold values from -0.4375 to 0.4375
- linear: float32 [512, 64, 192], P('scen', 'clus'), may hold values from -6 to 6
- arrival: int32 [512, 64], P('scen', 'clus'), may hold values from 0 to 47
- departure: int32 [512, 64], P('scen', 'clus'), may hold values from 48 to 96
- ev_count: int32 [64], P('clus'), may hold values from 8 to 48
- prob: float32 [512], P('scen'), may hold values from 0.5 to 13.5, as said below
- branch_of: int32 [512], P('scen'), may hold values from 0 to 7, as said below
- multiplier: float32 [512, 96], P('scen'), may hold values from -0.12 to 0.12
- root_prev: float32 [32], replicated, may hold values from -12 to 12
- branch_prev: float32 [8, 64], replicated, may hold values from -12 to 12
Outputs:
- power: float32 [512, 64, 192], P('scen', 'clus')
- bid: float32 [512, 96], P('scen')
- multiplier_next: float32 [512, 96], P('scen')
- node_mean: float32 [8, 96], replicated
- gap: float32 [], replicated
The draws below stay inside these ranges and needn't reach their ends.
Inputs may be any that keep to these rules, and one draw needn't show every extreme that they name: `branch_of`: each of the 8 branches holds exactly 64 scenarios. `prob`: positive.
All inputs are finite; a program needn't handle non-finite values.
Results may differ from the reference program's by a relative error of at most 0.0035.
Values may be sent and summed in bfloat16 or wider, within the bound.
A program may use at most 64 MiB of HBM per device.

```python
import jax
import jax.numpy as jnp
from jax import lax

QH = 96
BLOCK = 192
SPLIT = 32
BRANCHES = 8
SCENARIOS = 512
CLUSTERS = 64


def draw_prob(key, part):
    position = jnp.arange(SCENARIOS, dtype=jnp.float32)
    rising = 1.0 + 2.0 * position / max(SCENARIOS - 1, 1)
    spread_part = jax.random.uniform(key, (SCENARIOS,), jnp.float32, 0.5, 1.5)
    values = rising * spread_part
    return values.astype(jnp.float32)


def draw_branch_of(key, part):
    shuffled = jax.random.permutation(jax.random.fold_in(key, 7), SCENARIOS)
    return (shuffled % BRANCHES).astype(jnp.int32)


def touch_ends(result, own_key, least, top_value):
    extent = result.shape
    place = [jax.random.randint(jax.random.fold_in(own_key, axis), (), 0, extent[axis]) for axis in range(len(extent))]
    result = result.at[tuple(place)].set(least)
    longest = extent.index(max(extent))
    place[longest] = (place[longest] + 1) % extent[longest]
    return result.at[tuple(place)].set(top_value)


def block_levels(key, extent, pieces, least, high):
    level = 1.0
    for dim, parts in pieces:
        heights = jax.random.uniform(jax.random.fold_in(jax.random.fold_in(key, 6), dim), (parts,), jnp.float32, least / len(pieces), high / len(pieces))
        level = level * jnp.repeat(jnp.exp(heights), extent[dim] // parts).reshape((-1,) + (1,) * (len(extent) - 1 - dim))
    return level


def noise(rng, dims, scale, limit, shards=(), kind=jnp.bfloat16):
    entries = jax.random.normal(rng, dims, jnp.float32) * scale
    if len(shards) > 0:
        entries = block_levels(rng, dims, shards, -0.22, 0.18) * entries
    return jnp.clip(entries, min=-limit, max=limit).astype(kind)


def setup_inputs(seed: int = 0) -> dict:
    key_list = jax.random.split(jax.random.key(seed), 11)
    return {
        "factors": noise(key_list[0], (SCENARIOS, CLUSTERS, BLOCK * BLOCK), BLOCK ** -0.5, 0.4375, ((0, 32), (1, 16))),
        "linear": noise(key_list[1], (SCENARIOS, CLUSTERS, BLOCK), 1.0, 6.0, ((0, 32), (1, 16)), jnp.float32),
        "arrival": touch_ends(jax.random.randint(key_list[2], (SCENARIOS, CLUSTERS), 0, QH // 2), jax.random.fold_in(key_list[2], 1), 0, (QH // 2) - 1).astype(jnp.int32),
        "departure": touch_ends(jax.random.randint(key_list[3], (SCENARIOS, CLUSTERS), QH // 2, QH + 1), jax.random.fold_in(key_list[3], 1), QH // 2, QH).astype(jnp.int32),
        "ev_count": touch_ends(jax.random.randint(key_list[4], (CLUSTERS,), 8, 49), jax.random.fold_in(key_list[4], 1), 8, 48).astype(jnp.int32),
        "prob": draw_prob(jax.random.fold_in(key_list[10], 71), 0),
        "branch_of": draw_branch_of(jax.random.fold_in(key_list[10], 71), 0),
        "multiplier": noise(key_list[7], (SCENARIOS, QH), 0.02, 0.12, ((0, 32),), jnp.float32),
        "root_prev": noise(key_list[8], (SPLIT,), 2.0, 12.0, (), jnp.float32),
        "branch_prev": noise(key_list[9], (BRANCHES, QH - SPLIT), 2.0, 12.0, (), jnp.float32),
    }


def node_statistics(weighted, masses, split_at):
    root_mean = jnp.sum(weighted, axis=0) / jnp.sum(masses)
    branch_mean = weighted / masses[:, None]
    columns = jnp.arange(weighted.shape[1], dtype=jnp.int32)
    return jnp.where((columns < split_at)[None, :], root_mean[None, :], branch_mean)

def rounded(values):
    return lax.optimization_barrier(values.astype(jnp.bfloat16)).astype(jnp.float32)

def reference(factors, linear, arrival, departure, ev_count, prob, branch_of, multiplier, root_prev, branch_prev):
    highest = lax.Precision.HIGHEST
    penalty = 1.0 / CLUSTERS
    onehot = (branch_of[:, None] == jnp.arange(BRANCHES, dtype=jnp.int32)[None, :]).astype(jnp.float32)
    anchor_tail = jnp.dot(onehot, branch_prev, precision=highest)
    anchor = jnp.concatenate([jnp.broadcast_to(root_prev[None, :], (SCENARIOS, SPLIT)), anchor_tail], axis=1)
    counts = ev_count.astype(jnp.float32) / 16.0

    def scenario(scenario_items):
        fac, lin, arr, dep, mult, anch = scenario_items
        widened = fac.astype(jnp.float32).reshape(CLUSTERS, BLOCK, BLOCK)
        quarter = jnp.arange(QH, dtype=jnp.int32)
        inside = ((quarter[None, :] >= arr[:, None]) & (quarter[None, :] < dep[:, None])).astype(jnp.float32)
        scaled = inside * counts[:, None]
        effective = rounded(lin * jnp.concatenate([scaled, scaled], axis=1))
        gram = jnp.einsum('ckt,cku->tu', widened, widened, precision=highest)
        schur = gram[:QH, :QH] - gram[:QH, QH:] - gram[QH:, :QH] + gram[QH:, QH:]
        pushed = jnp.einsum('ckj,cj->ck', widened, effective, precision=highest)
        pushed_half = rounded(pushed)
        back = jnp.einsum('ckj,ck->j', widened, pushed_half, precision=highest)
        offset = back[:QH] - back[QH:]
        system = jnp.eye(QH, dtype=jnp.float32) + penalty * schur
        lower_fac = jnp.linalg.cholesky(system)
        prices = jax.scipy.linalg.cho_solve((lower_fac, True), mult - penalty * (offset + anch))
        bid_one = -offset - jnp.dot(schur, prices, precision=highest)
        prices_half = rounded(prices)
        signed = jnp.concatenate([prices_half, -prices_half])
        moved = pushed + jnp.einsum('ckj,j->ck', widened, signed, precision=highest)
        moved_half = rounded(moved)
        power_one = -jnp.einsum('ckj,ck->cj', widened, moved_half, precision=highest)
        return (power_one, bid_one)
    power, bid = lax.map(scenario, (factors, linear, arrival, departure, multiplier, anchor))
    weighted = jnp.einsum('sb,st->bt', onehot, prob[:, None] * bid, precision=highest)
    masses = jnp.einsum('sb,s->b', onehot, prob, precision=highest)
    node_mean = node_statistics(weighted, masses, SPLIT)
    target = jnp.dot(onehot, node_mean, precision=highest)
    multiplier_next = multiplier + penalty * (bid - target)
    distance = bid - target
    gap = jnp.sum(prob * jnp.sum(distance * distance, axis=1)) / (QH * jnp.sum(prob))
    return (power, bid, multiplier_next, node_mean, gap)
```

```python
import functools

import jax
import jax.numpy as jnp
from jax import lax
from jax.experimental import pallas as pl
from jax.experimental.pallas import tpu as pltpu
from jax.sharding import PartitionSpec as P

MESH = pl.DeviceIdType.MESH
HALVES = 2
LANES = 128
F32 = jnp.float32
BF16 = jnp.bfloat16


def iota(shape, axis):
    return lax.broadcasted_iota(jnp.int32, shape, axis)


def dot_nt(a, b):
    return lax.dot_general(a, b, (((1,), (1,)), ((), ())), preferred_element_type=F32)


def eliminate(system, quarter):
    lane = iota((1, LANES), 1)

    def trip(_, matrix):
        for p in range(8):
            row = matrix[p : p + 1, :]
            inv = 1.0 / row[:, p : p + 1]
            weight = jnp.where(lane == p, 1.0 - inv, row * inv)
            matrix = matrix - matrix[:, p : p + 1] * weight
        matrix = jnp.concatenate([matrix[8:quarter], matrix[:8], matrix[quarter:]], axis=0)
        return pltpu.roll(matrix, LANES - 8, 1)

    return lax.fori_loop(0, quarter // 8, trip, system)


def kernel(
    n_scen,
    n_clus,
    clus_here,
    quarter,
    split_at,
    branch_count,
    x_hbm,
    lin_ref,
    arr_ref,
    dep_ref,
    ev_ref,
    prob_ref,
    branch_ref,
    mult_ref,
    root_ref,
    bprev_ref,
    power_ref,
    bid_ref,
    next_ref,
    mean_ref,
    gap_ref,
    xbuf,
    pt_buf,
    push_buf,
    e_even,
    e_odd,
    lhs_even,
    lhs_odd,
    table,
    send_m,
    send_v,
    recv_m,
    recv_v,
    msg,
    recv_p,
    stat,
    recv_s,
    x_sem,
    sm_sem,
    sv_sem,
    rm_sem,
    rv_sem,
    sp_sem,
    rp_sem,
    ss_sem,
    rs_sem,
):
    scen_here = n_clus
    half = quarter // 2
    width = 2 * quarter
    rows = quarter * clus_here
    inner = n_scen // HALVES
    plane = HALVES * n_clus
    penalty = 1.0 / (clus_here * n_clus)
    g = lax.axis_index("scen")
    me = lax.axis_index("clus")
    my_half = g // inner
    my_inner = lax.rem(g, inner)
    my_slot = my_half * n_clus + me

    def x_copy(s, t):
        return pltpu.make_async_copy(x_hbm.at[s, :, t], xbuf.at[s, t], x_sem.at[s, t])

    def start_x(k, carry):
        s = lax.rem(me + 1 + k, n_clus)
        for t in range(3):
            x_copy(s, t).start()
        return carry

    lax.fori_loop(0, scen_here, start_x, 0)

    barrier = pltpu.get_barrier_semaphore()

    def plane_device(slot):
        return ((slot // n_clus) * inner + my_inner, lax.rem(slot, n_clus))

    def line_device(slot):
        return (my_half * inner + slot, me)

    def greet_plane(j, carry):
        pl.semaphore_signal(
            barrier, inc=1, device_id=plane_device(lax.rem(my_slot + j, plane)), device_id_type=MESH
        )
        return carry

    def greet_line(j, carry):
        pl.semaphore_signal(
            barrier, inc=1, device_id=line_device(lax.rem(my_inner + j, inner)), device_id_type=MESH
        )
        return carry

    lax.fori_loop(1, plane, greet_plane, 0)
    lax.fori_loop(1, inner, greet_line, 0)

    t_index = iota((quarter, 2 * LANES), 0)
    l_index = iota((quarter, 2 * LANES), 1)
    even = jnp.where(l_index == t_index, 1.0, 0.0) - jnp.where(l_index == t_index + quarter, 1.0, 0.0)
    shifted = t_index + LANES // 2
    odd = jnp.where(l_index == shifted, 1.0, 0.0) - jnp.where(l_index == shifted + quarter, 1.0, 0.0)
    lhs_even[0:quarter, :] = even.astype(BF16)
    lhs_odd[0:quarter, :] = odd.astype(BF16)

    lane2 = iota((8, 2 * LANES), 1)
    hour = jnp.where(lane2 < quarter, lane2, lane2 - quarter)
    sub2 = iota((8, 2 * LANES), 0)
    count = jnp.zeros((8, 2 * LANES), F32)
    for c in range(clus_here):
        count = jnp.where(sub2 == c, ev_ref[c].astype(F32) / 16.0, count)

    def costs(s, carry):
        first = jnp.zeros((8, 2 * LANES), jnp.int32)
        last = jnp.zeros((8, 2 * LANES), jnp.int32)
        for c in range(clus_here):
            first = jnp.where(sub2 == c, arr_ref[s, c], first)
            last = jnp.where(sub2 == c, dep_ref[s, c], last)
        inside = jnp.where((hour >= first) & (hour < last), 1.0, 0.0)
        scaled = inside * count
        cost = jnp.concatenate(
            [lin_ref[s], jnp.zeros((clus_here, 2 * LANES - width), F32)], axis=1
        )
        cost = jnp.concatenate([cost, jnp.zeros((8 - clus_here, 2 * LANES), F32)], axis=0)
        value = cost * scaled
        pad = jnp.zeros((8, 2 * LANES), F32)
        e_even[s] = jnp.concatenate([value, pad], axis=0).astype(BF16)
        turned = pltpu.roll(value, LANES // 2, 1)
        e_odd[s] = jnp.concatenate([turned, pad], axis=0).astype(BF16)
        return carry

    lax.fori_loop(0, scen_here, costs, 0)

    def m_copy(dest, slot, sem_slot):
        return pltpu.make_async_remote_copy(
            src_ref=send_m.at[dest],
            dst_ref=recv_m.at[slot],
            send_sem=sm_sem.at[dest],
            recv_sem=rm_sem.at[sem_slot],
            device_id=(g, dest),
            device_id_type=MESH,
        )

    def v_copy(dest, slot, sem_slot):
        return pltpu.make_async_remote_copy(
            src_ref=send_v.at[dest],
            dst_ref=recv_v.at[slot],
            send_sem=sv_sem.at[dest],
            recv_sem=rv_sem.at[sem_slot],
            device_id=(g, dest),
            device_id_type=MESH,
        )

    row_of = lax.rem(iota((8, rows), 1), clus_here) == iota((8, rows), 0)
    diag_of = iota((quarter, LANES), 0) == iota((quarter, LANES), 1)
    below = iota((half, LANES), 1) < iota((half, LANES), 0)

    def local(k, carry):
        s = lax.rem(me + 1 + k, n_clus)
        for t in range(3):
            x_copy(s, t).wait()
        a = xbuf[s, 0].reshape(rows, LANES)
        b = xbuf[s, 1].reshape(rows, LANES)
        c = xbuf[s, 2].reshape(rows, LANES)
        lhs_even[quarter : quarter + 16, :] = e_even[s]
        lhs_odd[quarter : quarter + 16, :] = e_odd[s]
        part_even = dot_nt(lhs_even[...], jnp.concatenate([a, b], axis=1))
        part_odd = dot_nt(lhs_odd[...], jnp.concatenate([b, c], axis=1))
        pushed_even = jnp.sum(
            jnp.where(row_of, part_even[quarter : quarter + 8], 0.0), axis=0, keepdims=True
        )
        pushed_odd = jnp.sum(
            jnp.where(row_of, part_odd[quarter : quarter + 8], 0.0), axis=0, keepdims=True
        )
        pushed = jnp.concatenate([pushed_even, pushed_odd], axis=1)
        push_buf[s] = pushed
        paired = jnp.concatenate([part_even[:quarter], part_odd[:quarter]], axis=1).astype(BF16)
        pt_buf[s] = paired
        pushed_rows = jnp.broadcast_to(pushed, (16, 2 * rows)).astype(BF16)
        left = jnp.concatenate([paired, pushed_rows], axis=0)
        right = jnp.concatenate([left, jnp.zeros((16, 2 * rows), BF16)], axis=0)
        product = dot_nt(left, right)
        schur = product[:quarter]
        low = pltpu.roll(schur[half:], LANES - half, 1)
        send_m[s] = jnp.where(below, low, schur[:half]).astype(BF16)
        send_v[s, 0:1, :] = product[quarter : quarter + 1]
        send_v[s, 1:2, :] = jnp.sum(jnp.where(diag_of, schur, 0.0), axis=0, keepdims=True)

        @pl.when(k == 0)
        def _():
            pl.semaphore_wait(barrier, plane - 1 + inner - 1)

        @pl.when(k < scen_here - 1)
        def _():
            m_copy(s, me, me).start()
            v_copy(s, me, me).start()

        return carry

    lax.fori_loop(0, scen_here, local, 0)

    def gather(j, carry):
        mat, vec = carry
        source = lax.rem(me + n_clus - j, n_clus)
        m_copy(source, source, source).wait_recv()
        v_copy(source, source, source).wait_recv()
        return (mat + recv_m[source].astype(F32), vec + recv_v[source])

    mat, vec = lax.fori_loop(1, n_clus, gather, (send_m[me].astype(F32), send_v[me]))

    lane_h = iota((half, LANES), 1)
    row_h = iota((half, LANES), 0)
    flipped = jnp.concatenate([mat, jnp.zeros((LANES - half, LANES), F32)], axis=0).T
    flip_a = flipped[:half]
    top = jnp.where(lane_h > row_h, mat, flip_a)
    low = jnp.where(lane_h < row_h, mat, flip_a)
    low = pltpu.roll(low, half, 1)
    bottom = jnp.where(lane_h < half, flipped[half:quarter], low)
    schur = jnp.concatenate([top, bottom], axis=0)
    lane_q = iota((quarter, LANES), 1)
    schur = jnp.where(diag_of, vec[1:2], schur)
    system = jnp.where(diag_of, 1.0 + penalty * schur, penalty * schur)
    system = jnp.where(lane_q < quarter, system, 0.0)

    lane1 = iota((1, LANES), 1)
    branch = branch_ref[me]
    table[...] = jnp.zeros((8, LANES), F32)
    table[:, 0:split_at] = jnp.broadcast_to(root_ref[...], (8, split_at))
    table[:, split_at:quarter] = bprev_ref[...]
    anchor = jnp.sum(
        jnp.where(iota((8, LANES), 0) == branch, table[...], 0.0), axis=0, keepdims=True
    )
    mult = jnp.concatenate(
        [mult_ref[pl.ds(me, 1), :], jnp.zeros((1, LANES - quarter), F32)], axis=1
    )
    side = jnp.where(lane1 < quarter, mult - penalty * (vec[0:1] + anchor), 0.0)
    side_rows = jnp.where(iota((8, LANES), 0) == 0, side, 0.0)
    solved = eliminate(jnp.concatenate([system, side_rows], axis=0), quarter)
    prices = pltpu.roll(solved[quarter:], quarter, 1)[0:1]
    bid = anchor + (prices - mult) / penalty
    msg[0:1, :] = prices
    tail = jnp.where(lane1 == quarter, prob_ref[me], jnp.where(lane1 == quarter + 1, branch.astype(F32), 0.0))
    msg[1:2, :] = jnp.where(lane1 < quarter, bid, tail)
    recv_p[my_slot] = msg[...]

    def p_copy(slot, at):
        return pltpu.make_async_remote_copy(
            src_ref=msg,
            dst_ref=recv_p.at[at],
            send_sem=sp_sem.at[slot],
            recv_sem=rp_sem.at[at],
            device_id=plane_device(slot),
            device_id_type=MESH,
        )

    def send_p(j, carry):
        p_copy(lax.rem(my_slot + j, plane), my_slot).start()
        return carry

    lax.fori_loop(1, plane, send_p, 0)

    def wait_p(j, carry):
        slot = lax.rem(my_slot + plane - j, plane)
        p_copy(slot, slot).wait_recv()
        return carry

    lax.fori_loop(1, plane, wait_p, 0)

    lane_p = iota((plane, LANES), 1)
    raw = recv_p[:, 1, :]
    chance = raw[:, quarter : quarter + 1]
    group = raw[:, quarter + 1 : quarter + 2]
    bids = jnp.where(lane_p < quarter, raw, jnp.where(lane_p == quarter, 1.0, 0.0))
    centre = jnp.zeros((plane, LANES), F32)
    for b in range(branch_count):
        member = group == float(b)
        total = jnp.sum(jnp.where(member, chance * bids, 0.0), axis=0, keepdims=True)
        mass = total[:, quarter : quarter + 1]
        mean = jnp.where(mass > 0.0, total / jnp.where(mass > 0.0, mass, 1.0), 0.0)
        centre = jnp.where(member, mean, centre)
        stat[b : b + 1, :] = total
    away = bids - centre
    stat[8:9, :] = jnp.sum(chance * (away * away), axis=0, keepdims=True)
    stat[9:16, :] = jnp.zeros((7, LANES), F32)
    recv_s[my_inner] = stat[...]

    def s_copy(slot, at):
        return pltpu.make_async_remote_copy(
            src_ref=stat,
            dst_ref=recv_s.at[at],
            send_sem=ss_sem.at[slot],
            recv_sem=rs_sem.at[at],
            device_id=line_device(slot),
            device_id_type=MESH,
        )

    def send_s(j, carry):
        s_copy(lax.rem(my_inner + j, inner), my_inner).start()
        return carry

    lax.fori_loop(1, inner, send_s, 0)

    def powers(s, carry):
        price = recv_p[my_half * n_clus + s, 0:1, :][:, :quarter]
        price = jnp.broadcast_to(price, (16, quarter)).astype(BF16)
        step = jnp.dot(price, pt_buf[s], preferred_element_type=F32)
        moved = push_buf[s] + step[0:1]
        stacked = jnp.concatenate(
            [
                jnp.where(row_of, moved[:, :rows], 0.0)[:clus_here],
                jnp.where(row_of, moved[:, rows:], 0.0)[:clus_here],
                jnp.zeros((16 - 2 * clus_here, rows), F32),
            ],
            axis=0,
        ).astype(BF16)
        blocks = jnp.concatenate([xbuf[s, t].reshape(rows, LANES) for t in range(3)], axis=1)
        out = jnp.dot(stacked, blocks, preferred_element_type=F32)
        from_odd = pltpu.roll(out[clus_here : 2 * clus_here, LANES:], LANES + LANES // 2, 1)
        total = out[:clus_here, : 2 * LANES] + from_odd
        power_ref[s] = -total[:, :width]
        return carry

    lax.fori_loop(0, scen_here, powers, 0)

    def wait_s(j, carry):
        slot = lax.rem(my_inner + inner - j, inner)
        s_copy(slot, slot).wait_recv()
        return carry

    lax.fori_loop(1, inner, wait_s, 0)

    lane8 = iota((8, LANES), 1)
    weighted = recv_s[0, 0:8, :]
    for j in range(1, inner):
        weighted = weighted + recv_s[j, 0:8, :]
    masses = weighted[:, quarter : quarter + 1]
    whole = jnp.sum(weighted, axis=0, keepdims=True)
    whole_mass = whole[:, quarter : quarter + 1]
    mean = jnp.where(lane8 < split_at, whole / whole_mass, weighted / masses)
    mean_ref[...] = mean[:, :quarter]
    spread = jnp.zeros((8, LANES), F32)
    within = jnp.zeros((1, LANES), F32)
    for j in range(inner):
        part = recv_s[j, 0:8, :]
        mass = part[:, quarter : quarter + 1]
        here = mass > 0.0
        away = jnp.where(here, part / jnp.where(here, mass, 1.0) - mean, 0.0)
        spread = spread + mass * (away * away)
        within = within + recv_s[j, 8:9, :]
    spread = jnp.where(lane8 < quarter, spread, 0.0)
    within = jnp.where(lane1 < quarter, within, 0.0)
    both = jnp.sum(spread, axis=0, keepdims=True) + within
    gap_ref[...] = jnp.sum(both, axis=1, keepdims=True) / (quarter * whole_mass)

    mine = recv_p[pl.ds(my_half * n_clus, n_clus), 1, :]
    group = mine[:, quarter + 1 : quarter + 2]
    target = jnp.zeros((n_clus, LANES), F32)
    for b in range(branch_count):
        target = jnp.where(group == float(b), mean[b : b + 1], target)
    bid_ref[...] = mine[:, :quarter]
    next_ref[...] = mult_ref[...] + penalty * (mine - target)[:, :quarter]

    def drain_m(j, carry):
        dest = lax.rem(me + j, n_clus)
        m_copy(dest, me, me).wait_send()
        v_copy(dest, me, me).wait_send()
        return carry

    def drain_p(j, carry):
        p_copy(lax.rem(my_slot + j, plane), my_slot).wait_send()
        return carry

    def drain_s(j, carry):
        s_copy(lax.rem(my_inner + j, inner), my_inner).wait_send()
        return carry

    lax.fori_loop(1, n_clus, drain_m, 0)
    lax.fori_loop(1, plane, drain_p, 0)
    lax.fori_loop(1, inner, drain_s, 0)


def solution(mesh):
    n_scen, n_clus = mesh.shape["scen"], mesh.shape["clus"]

    def step(
        factors,
        linear,
        arrival,
        departure,
        ev_count,
        prob,
        branch_of,
        multiplier,
        root_prev,
        branch_prev,
    ):
        scen_here, clus_here = factors.shape[:2]
        width = linear.shape[2]
        quarter = multiplier.shape[1]
        split_at = root_prev.shape[0]
        branch_count = branch_prev.shape[0]
        rows = quarter * clus_here
        plane = HALVES * n_clus
        inner = n_scen // HALVES
        tiles = factors.reshape(scen_here, clus_here, quarter, 3, LANES).transpose(0, 2, 3, 1, 4)
        vmem = pl.BlockSpec(memory_space=pltpu.VMEM)
        smem = pl.BlockSpec(memory_space=pltpu.SMEM)
        dma = pltpu.SemaphoreType.DMA
        power, bid, following, mean, gap = pl.pallas_call(
            functools.partial(
                kernel, n_scen, n_clus, clus_here, quarter, split_at, branch_count
            ),
            out_shape=(
                jax.ShapeDtypeStruct((scen_here, clus_here, width), F32),
                jax.ShapeDtypeStruct((scen_here, quarter), F32),
                jax.ShapeDtypeStruct((scen_here, quarter), F32),
                jax.ShapeDtypeStruct((branch_count, quarter), F32),
                jax.ShapeDtypeStruct((1, 1), F32),
            ),
            in_specs=[
                pl.BlockSpec(memory_space=pl.ANY),
                vmem,
                smem,
                smem,
                smem,
                smem,
                smem,
                vmem,
                vmem,
                vmem,
            ],
            out_specs=(vmem,) * 5,
            scratch_shapes=[
                pltpu.VMEM((scen_here, 3, quarter, clus_here, LANES), BF16),
                pltpu.VMEM((scen_here, quarter, 2 * rows), BF16),
                pltpu.VMEM((scen_here, 1, 2 * rows), F32),
                pltpu.VMEM((scen_here, 16, 2 * LANES), BF16),
                pltpu.VMEM((scen_here, 16, 2 * LANES), BF16),
                pltpu.VMEM((quarter + 16, 2 * LANES), BF16),
                pltpu.VMEM((quarter + 16, 2 * LANES), BF16),
                pltpu.VMEM((8, LANES), F32),
                pltpu.VMEM((n_clus, quarter // 2, LANES), BF16),
                pltpu.VMEM((n_clus, 2, LANES), F32),
                pltpu.VMEM((n_clus, quarter // 2, LANES), BF16),
                pltpu.VMEM((n_clus, 2, LANES), F32),
                pltpu.VMEM((2, LANES), F32),
                pltpu.VMEM((plane, 2, LANES), F32),
                pltpu.VMEM((16, LANES), F32),
                pltpu.VMEM((inner, 16, LANES), F32),
                dma((scen_here, 3)),
                dma((n_clus,)),
                dma((n_clus,)),
                dma((n_clus,)),
                dma((n_clus,)),
                dma((plane,)),
                dma((plane,)),
                dma((inner,)),
                dma((inner,)),
            ],
            compiler_params=pltpu.CompilerParams(collective_id=0, has_side_effects=True),
        )(
            tiles,
            linear,
            arrival,
            departure,
            ev_count,
            prob,
            branch_of,
            multiplier,
            root_prev[None, :],
            branch_prev,
        )
        return (power, bid, following, mean, gap.reshape(()))

    return jax.shard_map(
        step,
        mesh=mesh,
        in_specs=(
            P("scen", "clus", None),
            P("scen", "clus", None),
            P("scen", "clus"),
            P("scen", "clus"),
            P("clus"),
            P("scen"),
            P("scen"),
            P("scen", None),
            P(),
            P(),
        ),
        out_specs=(P("scen", "clus", None), P("scen", None), P("scen", None), P(), P()),
        check_vma=False,
    )
```

```python
import functools

import jax
import jax.numpy as jnp
from jax import lax
from jax.experimental import pallas as pl
from jax.experimental.pallas import tpu as pltpu
from jax.sharding import PartitionSpec as P

MESH = pl.DeviceIdType.MESH
HALVES = 2
LANES = 128
F32 = jnp.float32
BF16 = jnp.bfloat16


def iota(shape, axis):
    return lax.broadcasted_iota(jnp.int32, shape, axis)


def dot_nt(a, b):
    return lax.dot_general(a, b, (((1,), (1,)), ((), ())), preferred_element_type=F32)


def spread_row(tile, p):
    return jnp.broadcast_to(tile[p : p + 1, :], (8, LANES))


def eliminate(system, quarter):
    height = quarter + 8
    lane = iota((8, LANES), 1)
    sub = iota((8, LANES), 0)
    lane_all = iota((height, LANES), 1)

    def trip(k, matrix):
        base = 8 * k
        columns = [
            jnp.take_along_axis(matrix, jnp.full((height, LANES), base + q, jnp.int32), axis=1)
            for q in range(8)
        ]
        block = matrix[:8]
        own = [column[:8] for column in columns]
        for p in range(8):
            here = sub == p
            inv = 1.0 / spread_row(own[p], p)
            factor = jnp.where(here, 0.0, own[p])
            for q in range(p + 1, 8):
                scaled = spread_row(own[q], p) * inv
                own[q] = jnp.where(here, scaled, own[q] - factor * scaled)
            scaled = spread_row(block, p) * inv
            block = jnp.where(here, scaled, block - factor * scaled)
            block = jnp.where(lane == base + p, jnp.where(here, inv, -own[p] * inv), block)
        weight = jnp.where((lane >= base) & (lane < base + 8), -block, block)
        taken = (lane_all >= base) & (lane_all < base + 8)
        terms = [
            columns[q] * jnp.broadcast_to(weight[q : q + 1, :], (height, LANES)) for q in range(8)
        ]
        while len(terms) > 1:
            terms = [terms[i] + terms[i + 1] for i in range(0, len(terms), 2)]
        matrix = jnp.where(taken, 0.0, matrix) - terms[0]
        return jnp.concatenate([matrix[8:quarter], matrix[:8], matrix[quarter:]], axis=0)

    return lax.fori_loop(0, quarter // 8, trip, system)


def kernel(
    n_scen,
    n_clus,
    clus_here,
    quarter,
    split_at,
    branch_count,
    x_hbm,
    lin_hbm,
    arr_hbm,
    dep_hbm,
    ev_hbm,
    prob_hbm,
    branch_hbm,
    mult_hbm,
    root_hbm,
    bprev_hbm,
    power_ref,
    bid_ref,
    next_ref,
    mean_ref,
    gap_ref,
    xbuf,
    lin_ref,
    arr_ref,
    dep_ref,
    ev_ref,
    prob_ref,
    branch_ref,
    mult_ref,
    root_ref,
    bprev_ref,
    pt_buf,
    push_buf,
    lhs_even,
    lhs_odd,
    table,
    chance,
    send_m,
    send_v,
    recv_m,
    recv_v,
    send_t,
    recv_t,
    msg,
    recv_p,
    stat,
    recv_s,
    small_sem,
    x_sem,
    send_sem,
    recv_sem,
):
    scen_here = n_clus
    half = quarter // 2
    width = 2 * quarter
    rows = quarter * clus_here
    inner = n_scen // HALVES
    plane = HALVES * n_clus
    penalty = 1.0 / (clus_here * n_clus)
    g = lax.axis_index("scen")
    me = lax.axis_index("clus")
    my_half = g // inner
    my_inner = lax.rem(g, inner)
    my_slot = my_half * n_clus + me
    my_base = my_half * n_clus
    other = 1 - my_half

    barrier = pltpu.get_barrier_semaphore()

    def plane_device(slot):
        return ((slot // n_clus) * inner + my_inner, lax.rem(slot, n_clus))

    def line_device(slot):
        return (my_half * inner + slot, me)

    def greet_plane(j, carry):
        pl.semaphore_signal(
            barrier, inc=1, device_id=plane_device(lax.rem(my_slot + j, plane)), device_id_type=MESH
        )
        return carry

    def greet_line(j, carry):
        pl.semaphore_signal(
            barrier, inc=1, device_id=line_device(lax.rem(my_inner + j, inner)), device_id_type=MESH
        )
        return carry

    small = [
        pltpu.make_async_copy(source, target, small_sem.at[i])
        for i, (source, target) in enumerate(
            (
                (lin_hbm, lin_ref),
                (arr_hbm, arr_ref),
                (dep_hbm, dep_ref),
                (ev_hbm, ev_ref),
                (prob_hbm, prob_ref),
                (branch_hbm, branch_ref),
                (mult_hbm, mult_ref),
                (root_hbm, root_ref),
                (bprev_hbm, bprev_ref),
            )
        )
    ]
    for copy in small:
        copy.start()

    def x_copy(s, t):
        return pltpu.make_async_copy(x_hbm.at[s, :, t], xbuf.at[s, t], x_sem.at[s, t])

    def start_x(k, carry):
        s = lax.rem(me + 1 + k, n_clus)
        for t in range(3):
            x_copy(s, t).start()
        return carry

    lax.fori_loop(0, scen_here, start_x, 0)
    lax.fori_loop(1, plane, greet_plane, 0)
    lax.fori_loop(1, inner, greet_line, 0)

    t_index = iota((quarter, 2 * LANES), 0)
    l_index = iota((quarter, 2 * LANES), 1)
    even = jnp.where(l_index == t_index, 1.0, 0.0) - jnp.where(l_index == t_index + quarter, 1.0, 0.0)
    shifted = t_index + LANES // 2
    odd = jnp.where(l_index == shifted, 1.0, 0.0) - jnp.where(l_index == shifted + quarter, 1.0, 0.0)
    lhs_even[...] = even.astype(BF16)
    lhs_odd[...] = odd.astype(BF16)

    for copy in small:
        copy.wait()

    lane2 = iota((8, 2 * LANES), 1)
    hour = jnp.where(lane2 < quarter, lane2, lane2 - quarter)
    sub2 = iota((8, 2 * LANES), 0)
    count = jnp.zeros((8, 2 * LANES), F32)
    for c in range(clus_here):
        count = jnp.where(sub2 == c, ev_ref[c].astype(F32) / 16.0, count)

    def costs(s):
        first = jnp.zeros((8, 2 * LANES), jnp.int32)
        last = jnp.zeros((8, 2 * LANES), jnp.int32)
        for c in range(clus_here):
            first = jnp.where(sub2 == c, arr_ref[c, s], first)
            last = jnp.where(sub2 == c, dep_ref[c, s], last)
        inside = jnp.where((hour >= first) & (hour < last), 1.0, 0.0)
        cost = jnp.concatenate(
            [lin_ref[s], jnp.zeros((clus_here, 2 * LANES - width), F32)], axis=1
        )
        cost = jnp.concatenate([cost, jnp.zeros((8 - clus_here, 2 * LANES), F32)], axis=0)
        value = cost * (inside * count)
        turned = pltpu.roll(value, LANES // 2, 1)
        pad = jnp.zeros((8, 2 * LANES), F32)
        return (
            jnp.concatenate([value, pad], axis=0).astype(BF16),
            jnp.concatenate([turned, pad], axis=0).astype(BF16),
        )

    def remote(source, target, kind, device):
        return pltpu.make_async_remote_copy(
            src_ref=source,
            dst_ref=target,
            send_sem=send_sem.at[kind],
            recv_sem=recv_sem.at[kind],
            device_id=device,
            device_id_type=MESH,
        )

    def await_all(buffer, kind, sems, amount):
        view = buffer.at[pl.ds(0, amount)]
        pltpu.make_async_copy(view, view, sems.at[kind]).wait()

    row_of = lax.rem(iota((8, rows), 1), clus_here) == iota((8, rows), 0)
    diag_of = iota((quarter, LANES), 0) == iota((quarter, LANES), 1)
    below = iota((half, LANES), 1) < iota((half, LANES), 0)
    lane1 = iota((1, LANES), 1)
    lane8 = iota((8, LANES), 1)
    sub8 = iota((8, LANES), 0)

    def tiles_of(s):
        return [xbuf.at[s, t].reshape(rows, LANES)[...] for t in range(3)]

    chances = jnp.zeros((1, LANES), F32)
    groups = jnp.zeros((1, LANES), F32)
    group_rows = jnp.zeros((n_clus, LANES), jnp.int32)
    sub_n = iota((n_clus, LANES), 0)
    for i in range(n_clus):
        chances = jnp.where(lane1 == i, prob_ref[i], chances)
        groups = jnp.where(lane1 == i, branch_ref[i].astype(F32), groups)
        group_rows = jnp.where(sub_n == i, branch_ref[i], group_rows)
        chance[my_base + i] = jnp.where(sub8 == branch_ref[i], prob_ref[i], 0.0)
    send_t[0:1, :] = chances
    send_t[1:2, :] = groups
    t_copy = remote(send_t, recv_t, 2, (other * inner + my_inner, me))

    def local(k, carry):
        s = lax.rem(me + 1 + k, n_clus)
        for t in range(3):
            x_copy(s, t).wait()
        a, b, c = tiles_of(s)
        cost_even, cost_odd = costs(s)
        part_even = dot_nt(
            jnp.concatenate([lhs_even[...], cost_even], axis=0), jnp.concatenate([a, b], axis=1)
        )
        part_odd = dot_nt(
            jnp.concatenate([lhs_odd[...], cost_odd], axis=0), jnp.concatenate([b, c], axis=1)
        )
        pushed_even = jnp.sum(
            jnp.where(row_of, part_even[quarter : quarter + 8], 0.0), axis=0, keepdims=True
        )
        pushed_odd = jnp.sum(
            jnp.where(row_of, part_odd[quarter : quarter + 8], 0.0), axis=0, keepdims=True
        )
        pushed = jnp.concatenate([pushed_even, pushed_odd], axis=1)
        push_buf[s] = pushed
        paired = jnp.concatenate([part_even[:quarter], part_odd[:quarter]], axis=1).astype(BF16)
        pt_buf[s] = paired
        pushed_rows = jnp.broadcast_to(pushed, (16, 2 * rows)).astype(BF16)
        left = jnp.concatenate([paired, pushed_rows], axis=0)
        right = jnp.concatenate([left, jnp.zeros((16, 2 * rows), BF16)], axis=0)
        product = dot_nt(left, right)
        schur = product[:quarter]
        low = pltpu.roll(schur[half:], LANES - half, 1)
        send_m[s] = jnp.where(below, low, schur[:half]).astype(BF16)
        send_v[s, 0:1, :] = product[quarter : quarter + 1]
        send_v[s, 1:2, :] = jnp.sum(jnp.where(diag_of, schur, 0.0), axis=0, keepdims=True)

        @pl.when(k == 0)
        def _():
            pl.semaphore_wait(barrier, plane - 1 + inner - 1)
            t_copy.start()

        @pl.when(k < scen_here - 1)
        def _():
            remote(send_m.at[s], recv_m.at[me], 0, (g, s)).start()
            remote(send_v.at[s], recv_v.at[me], 1, (g, s)).start()

        return carry

    lax.fori_loop(0, scen_here, local, 0)

    table[...] = jnp.zeros((8, LANES), F32)
    table[:, 0:split_at] = jnp.broadcast_to(root_ref[...], (8, split_at))
    table[:, split_at:quarter] = bprev_ref[...]
    branch = branch_ref[me]
    anchor = jnp.sum(jnp.where(sub8 == branch, table[...], 0.0), axis=0, keepdims=True)
    mult = jnp.concatenate(
        [mult_ref[pl.ds(me, 1), :], jnp.zeros((1, LANES - quarter), F32)], axis=1
    )
    t_copy.wait_recv()
    far_chance = recv_t[0:1, :]
    far_group = recv_t[1:2, :]
    for i in range(n_clus):
        member = sub8.astype(F32) == far_group[:, i : i + 1]
        chance[other * n_clus + i] = jnp.where(member, far_chance[:, i : i + 1], 0.0)
    mass = chance[0]
    for i in range(1, plane):
        mass = mass + chance[i]
    inv_mass = jnp.where(mass > 0.0, 1.0 / jnp.where(mass > 0.0, mass, 1.0), 0.0)

    recv_m[me] = send_m[me]
    recv_v[me] = send_v[me]
    await_all(recv_m, 0, recv_sem, n_clus - 1)
    await_all(recv_v, 1, recv_sem, n_clus - 1)
    mats = [recv_m[j].astype(F32) for j in range(n_clus)]
    vecs = [recv_v[j] for j in range(n_clus)]
    while len(mats) > 1:
        mats = [mats[i] + mats[i + 1] for i in range(0, len(mats), 2)]
        vecs = [vecs[i] + vecs[i + 1] for i in range(0, len(vecs), 2)]
    mat, vec = mats[0], vecs[0]

    lane_h = iota((half, LANES), 1)
    row_h = iota((half, LANES), 0)
    flipped = jnp.concatenate([mat, jnp.zeros((LANES - half, LANES), F32)], axis=0).T
    flip_a = flipped[:half]
    top = jnp.where(lane_h > row_h, mat, flip_a)
    low = jnp.where(lane_h < row_h, mat, flip_a)
    low = pltpu.roll(low, half, 1)
    bottom = jnp.where(lane_h < half, flipped[half:quarter], low)
    schur = jnp.concatenate([top, bottom], axis=0)
    lane_q = iota((quarter, LANES), 1)
    schur = jnp.where(diag_of, vec[1:2], schur)
    system = jnp.where(diag_of, 1.0 + penalty * schur, penalty * schur)
    system = jnp.where(lane_q < quarter, system, 0.0)
    side = jnp.where(lane1 < quarter, mult - penalty * (vec[0:1] + anchor), 0.0)
    side_rows = jnp.where(sub8 == 0, side, 0.0)
    solved = eliminate(jnp.concatenate([system, side_rows], axis=0), quarter)
    prices = solved[quarter : quarter + 1]
    bid = anchor + (prices - mult) / penalty
    msg[0:1, :] = prices
    msg[1:2, :] = jnp.where(lane1 < quarter, bid, jnp.where(lane1 == quarter, 1.0, 0.0))
    recv_p[my_slot] = msg[...]

    def send_p(j, carry):
        slot = lax.rem(my_slot + j, plane)
        remote(msg, recv_p.at[my_slot], 3, plane_device(slot)).start()
        return carry

    lax.fori_loop(1, plane, send_p, 0, unroll=True)
    await_all(recv_p, 3, recv_sem, plane - 1)

    def bid_tile(i):
        return jnp.broadcast_to(recv_p[i, 1:2, :], (8, LANES))

    totals = [chance[i] * bid_tile(i) for i in range(plane)]
    while len(totals) > 1:
        totals = [totals[i] + totals[i + 1] for i in range(0, len(totals), 2)]
    mean = totals[0] * inv_mass
    squares = []
    for i in range(plane):
        away = bid_tile(i) - mean
        squares.append(chance[i] * (away * away))
    while len(squares) > 1:
        squares = [squares[i] + squares[i + 1] for i in range(0, len(squares), 2)]
    square = jnp.sum(jnp.where(lane8 < quarter, squares[0], 0.0), axis=0, keepdims=True)
    square = jnp.sum(square, axis=1, keepdims=True)
    stat[...] = jnp.where(
        lane8 < quarter, mean, jnp.where(lane8 == quarter, mass, jnp.where(sub8 == 0, square, 0.0))
    )
    recv_s[my_inner] = stat[...]

    def send_s(j, carry):
        slot = lax.rem(my_inner + j, inner)
        remote(stat, recv_s.at[my_inner], 4, line_device(slot)).start()
        return carry

    lax.fori_loop(1, inner, send_s, 0, unroll=True)

    def powers(s, carry):
        price = recv_p[my_base + s, 0:1, :][:, :quarter]
        price = jnp.broadcast_to(price, (16, quarter)).astype(BF16)
        step = jnp.dot(price, pt_buf[s], preferred_element_type=F32)
        moved = push_buf[s] + step[0:1]
        stacked = jnp.concatenate(
            [
                jnp.where(row_of, moved[:, :rows], 0.0)[:clus_here],
                jnp.where(row_of, moved[:, rows:], 0.0)[:clus_here],
                jnp.zeros((16 - 2 * clus_here, rows), F32),
            ],
            axis=0,
        ).astype(BF16)
        out = jnp.dot(stacked, jnp.concatenate(tiles_of(s), axis=1), preferred_element_type=F32)
        from_odd = pltpu.roll(out[clus_here : 2 * clus_here, LANES:], LANES + LANES // 2, 1)
        total = out[:clus_here, : 2 * LANES] + from_odd
        power_ref[s] = -total[:, :width]
        return carry

    lax.fori_loop(0, scen_here, powers, 0, unroll=2)
    mine = recv_p[pl.ds(my_base, n_clus), 1, :]
    bid_ref[...] = mine[:, :quarter]
    await_all(send_m, 0, send_sem, n_clus - 1)
    await_all(send_v, 1, send_sem, n_clus - 1)
    t_copy.wait_send()
    await_all(recv_p, 3, send_sem, plane - 1)

    await_all(recv_s, 4, recv_sem, inner - 1)
    parts = [recv_s[j] for j in range(inner)]
    weights = [jnp.broadcast_to(part[:, quarter : quarter + 1], (8, LANES)) for part in parts]
    sums = [part * weight for part, weight in zip(parts, weights)]
    heavy = list(weights)
    while len(sums) > 1:
        sums = [sums[i] + sums[i + 1] for i in range(0, len(sums), 2)]
        heavy = [heavy[i] + heavy[i + 1] for i in range(0, len(heavy), 2)]
    whole = jnp.sum(sums[0], axis=0, keepdims=True)
    whole_mass = jnp.sum(heavy[0], axis=0, keepdims=True)
    node = jnp.where(lane8 < split_at, whole / whole_mass, sums[0] / heavy[0])
    mean_ref[...] = node[:, :quarter]
    target = jnp.zeros((n_clus, LANES), F32)
    for b in range(branch_count):
        target = jnp.where(group_rows == b, node[b : b + 1], target)
    next_ref[...] = mult_ref[...] + penalty * (mine - target)[:, :quarter]
    spread = []
    within = []
    for part, weight in zip(parts, weights):
        away = part - node
        spread.append(weight * (away * away))
        within.append(part[0:1])
    while len(spread) > 1:
        spread = [spread[i] + spread[i + 1] for i in range(0, len(spread), 2)]
        within = [within[i] + within[i + 1] for i in range(0, len(within), 2)]
    both = jnp.sum(jnp.where(lane8 < quarter, spread[0], 0.0), axis=0, keepdims=True)
    both = both + jnp.where(lane1 == quarter + 1, within[0], 0.0)
    gap_ref[...] = jnp.sum(both, axis=1, keepdims=True) / (quarter * whole_mass[:, 0:1])
    await_all(recv_s, 4, send_sem, inner - 1)


def solution(mesh):
    n_scen, n_clus = mesh.shape["scen"], mesh.shape["clus"]

    def step(
        factors,
        linear,
        arrival,
        departure,
        ev_count,
        prob,
        branch_of,
        multiplier,
        root_prev,
        branch_prev,
    ):
        scen_here, clus_here = factors.shape[:2]
        width = linear.shape[2]
        quarter = multiplier.shape[1]
        split_at = root_prev.shape[0]
        branch_count = branch_prev.shape[0]
        rows = quarter * clus_here
        plane = HALVES * n_clus
        inner = n_scen // HALVES
        tiles = factors.reshape(scen_here, clus_here, quarter, 3, LANES).transpose(0, 2, 3, 1, 4)
        vmem = pl.BlockSpec(memory_space=pltpu.VMEM)
        dma = pltpu.SemaphoreType.DMA
        power, bid, following, mean, gap = pl.pallas_call(
            functools.partial(
                kernel, n_scen, n_clus, clus_here, quarter, split_at, branch_count
            ),
            out_shape=(
                jax.ShapeDtypeStruct((scen_here, clus_here, width), F32),
                jax.ShapeDtypeStruct((scen_here, quarter), F32),
                jax.ShapeDtypeStruct((scen_here, quarter), F32),
                jax.ShapeDtypeStruct((branch_count, quarter), F32),
                jax.ShapeDtypeStruct((1, 1), F32),
            ),
            in_specs=[pl.BlockSpec(memory_space=pl.ANY)] * 10,
            out_specs=(vmem,) * 5,
            scratch_shapes=[
                pltpu.VMEM((scen_here, 3, quarter, clus_here, LANES), BF16),
                pltpu.VMEM(linear.shape, F32),
                pltpu.SMEM((clus_here, scen_here), jnp.int32),
                pltpu.SMEM((clus_here, scen_here), jnp.int32),
                pltpu.SMEM((clus_here,), jnp.int32),
                pltpu.SMEM((scen_here,), F32),
                pltpu.SMEM((scen_here,), jnp.int32),
                pltpu.VMEM(multiplier.shape, F32),
                pltpu.VMEM((1, split_at), F32),
                pltpu.VMEM(branch_prev.shape, F32),
                pltpu.VMEM((scen_here, quarter, 2 * rows), BF16),
                pltpu.VMEM((scen_here, 1, 2 * rows), F32),
                pltpu.VMEM((quarter, 2 * LANES), BF16),
                pltpu.VMEM((quarter, 2 * LANES), BF16),
                pltpu.VMEM((8, LANES), F32),
                pltpu.VMEM((plane, 8, LANES), F32),
                pltpu.VMEM((n_clus, quarter // 2, LANES), BF16),
                pltpu.VMEM((n_clus, 2, LANES), F32),
                pltpu.VMEM((n_clus, quarter // 2, LANES), BF16),
                pltpu.VMEM((n_clus, 2, LANES), F32),
                pltpu.VMEM((2, LANES), F32),
                pltpu.VMEM((2, LANES), F32),
                pltpu.VMEM((2, LANES), F32),
                pltpu.VMEM((plane, 2, LANES), F32),
                pltpu.VMEM((8, LANES), F32),
                pltpu.VMEM((inner, 8, LANES), F32),
                dma((9,)),
                dma((scen_here, 3)),
                dma((5,)),
                dma((5,)),
            ],
            compiler_params=pltpu.CompilerParams(collective_id=0, has_side_effects=True),
        )(
            tiles,
            linear,
            arrival.T,
            departure.T,
            ev_count,
            prob,
            branch_of,
            multiplier,
            root_prev[None, :],
            branch_prev,
        )
        return (power, bid, following, mean, gap.reshape(()))

    return jax.shard_map(
        step,
        mesh=mesh,
        in_specs=(
            P("scen", "clus", None),
            P("scen", "clus", None),
            P("scen", "clus"),
            P("scen", "clus"),
            P("clus"),
            P("scen"),
            P("scen"),
            P("scen", None),
            P(),
            P(),
        ),
        out_specs=(P("scen", "clus", None), P("scen", None), P("scen", None), P(), P()),
        check_vma=False,
    )
```

```python
import functools

import jax
import jax.numpy as jnp
from jax import lax
from jax.experimental import pallas as pl
from jax.experimental.pallas import tpu as pltpu
from jax.sharding import PartitionSpec as P

MESH = pl.DeviceIdType.MESH
HALVES = 2
LANES = 128
F32 = jnp.float32
BF16 = jnp.bfloat16


def iota(shape, axis):
    return lax.broadcasted_iota(jnp.int32, shape, axis)


def dot_nt(a, b):
    return lax.dot_general(a, b, (((1,), (1,)), ((), ())), preferred_element_type=F32)


def spread_row(tile, p):
    return jnp.broadcast_to(tile[p : p + 1, :], (8, LANES))


def eliminate(system, quarter):
    height = quarter + 8
    lane = iota((8, LANES), 1)
    sub = iota((8, LANES), 0)
    lane_all = iota((height, LANES), 1)

    def trip(k, matrix):
        base = 8 * k
        columns = [
            jnp.take_along_axis(matrix, jnp.full((height, LANES), base + q, jnp.int32), axis=1)
            for q in range(8)
        ]
        block = matrix[:8]
        own = [column[:8] for column in columns]
        for p in range(8):
            here = sub == p
            inv = 1.0 / spread_row(own[p], p)
            factor = jnp.where(here, 0.0, own[p])
            for q in range(p + 1, 8):
                scaled = spread_row(own[q], p) * inv
                own[q] = jnp.where(here, scaled, own[q] - factor * scaled)
            scaled = spread_row(block, p) * inv
            block = jnp.where(here, scaled, block - factor * scaled)
            block = jnp.where(lane == base + p, jnp.where(here, inv, -own[p] * inv), block)
        weight = jnp.where((lane >= base) & (lane < base + 8), -block, block)
        taken = (lane_all >= base) & (lane_all < base + 8)
        terms = [
            columns[q] * jnp.broadcast_to(weight[q : q + 1, :], (height, LANES)) for q in range(8)
        ]
        while len(terms) > 1:
            terms = [terms[i] + terms[i + 1] for i in range(0, len(terms), 2)]
        matrix = jnp.where(taken, 0.0, matrix) - terms[0]
        return jnp.concatenate([matrix[8:quarter], matrix[:8], matrix[quarter:]], axis=0)

    return lax.fori_loop(0, quarter // 8, trip, system)


def kernel(
    n_scen,
    n_clus,
    clus_here,
    quarter,
    split_at,
    branch_count,
    x_hbm,
    lin_hbm,
    arr_hbm,
    dep_hbm,
    ev_hbm,
    prob_hbm,
    branch_hbm,
    mult_hbm,
    root_hbm,
    bprev_hbm,
    power_ref,
    bid_ref,
    next_ref,
    mean_ref,
    gap_ref,
    xbuf,
    lin_ref,
    arr_ref,
    dep_ref,
    ev_ref,
    prob_ref,
    branch_ref,
    mult_ref,
    root_ref,
    bprev_ref,
    pt_buf,
    push_buf,
    lhs_even,
    lhs_odd,
    table,
    chance,
    send_m,
    send_v,
    recv_m,
    recv_v,
    send_t,
    recv_t,
    msg,
    recv_p,
    stat,
    recv_s,
    small_sem,
    x_sem,
    send_sem,
    recv_sem,
):
    scen_here = n_clus
    half = quarter // 2
    width = 2 * quarter
    rows = quarter * clus_here
    inner = n_scen // HALVES
    plane = HALVES * n_clus
    penalty = 1.0 / (clus_here * n_clus)
    g = lax.axis_index("scen")
    me = lax.axis_index("clus")
    my_half = g // inner
    my_inner = lax.rem(g, inner)
    my_slot = my_half * n_clus + me
    my_base = my_half * n_clus
    other = 1 - my_half

    barrier = pltpu.get_barrier_semaphore()

    def plane_device(slot):
        return ((slot // n_clus) * inner + my_inner, lax.rem(slot, n_clus))

    def line_device(slot):
        return (my_half * inner + slot, me)

    def greet_plane(j, carry):
        pl.semaphore_signal(
            barrier, inc=1, device_id=plane_device(lax.rem(my_slot + j, plane)), device_id_type=MESH
        )
        return carry

    def greet_line(j, carry):
        pl.semaphore_signal(
            barrier, inc=1, device_id=line_device(lax.rem(my_inner + j, inner)), device_id_type=MESH
        )
        return carry

    small = [
        pltpu.make_async_copy(source, target, small_sem.at[i])
        for i, (source, target) in enumerate(
            (
                (lin_hbm, lin_ref),
                (arr_hbm, arr_ref),
                (dep_hbm, dep_ref),
                (ev_hbm, ev_ref),
                (prob_hbm, prob_ref),
                (branch_hbm, branch_ref),
                (mult_hbm, mult_ref),
                (root_hbm, root_ref),
                (bprev_hbm, bprev_ref),
            )
        )
    ]
    for copy in small:
        copy.start()

    def x_copy(s):
        return pltpu.make_async_copy(x_hbm.at[s], xbuf.at[s], x_sem.at[s])

    def start_x(k, carry):
        x_copy(lax.rem(me + 1 + k, n_clus)).start()
        return carry

    lax.fori_loop(0, scen_here, start_x, 0)
    lax.fori_loop(1, plane, greet_plane, 0)
    lax.fori_loop(1, inner, greet_line, 0)

    t_index = iota((quarter, 2 * LANES), 0)
    l_index = iota((quarter, 2 * LANES), 1)
    even = jnp.where(l_index == t_index, 1.0, 0.0) - jnp.where(l_index == t_index + quarter, 1.0, 0.0)
    shifted = t_index + LANES // 2
    odd = jnp.where(l_index == shifted, 1.0, 0.0) - jnp.where(l_index == shifted + quarter, 1.0, 0.0)
    lhs_even[...] = even.astype(BF16)
    lhs_odd[...] = odd.astype(BF16)

    for copy in small:
        copy.wait()

    lane2 = iota((8, 2 * LANES), 1)
    hour = jnp.where(lane2 < quarter, lane2, lane2 - quarter)
    sub2 = iota((8, 2 * LANES), 0)
    count = jnp.zeros((8, 2 * LANES), F32)
    for c in range(clus_here):
        count = jnp.where(sub2 == c, ev_ref[c].astype(F32) / 16.0, count)

    def costs(s):
        first = jnp.zeros((8, 2 * LANES), jnp.int32)
        last = jnp.zeros((8, 2 * LANES), jnp.int32)
        for c in range(clus_here):
            first = jnp.where(sub2 == c, arr_ref[c, s], first)
            last = jnp.where(sub2 == c, dep_ref[c, s], last)
        inside = jnp.where((hour >= first) & (hour < last), 1.0, 0.0)
        cost = jnp.concatenate(
            [lin_ref[s], jnp.zeros((clus_here, 2 * LANES - width), F32)], axis=1
        )
        cost = jnp.concatenate([cost, jnp.zeros((8 - clus_here, 2 * LANES), F32)], axis=0)
        value = cost * (inside * count)
        turned = pltpu.roll(value, LANES // 2, 1)
        pad = jnp.zeros((8, 2 * LANES), F32)
        return (
            jnp.concatenate([value, pad], axis=0).astype(BF16),
            jnp.concatenate([turned, pad], axis=0).astype(BF16),
        )

    def remote(source, target, kind, device):
        return pltpu.make_async_remote_copy(
            src_ref=source,
            dst_ref=target,
            send_sem=send_sem.at[kind],
            recv_sem=recv_sem.at[kind],
            device_id=device,
            device_id_type=MESH,
        )

    def await_all(buffer, kind, sems, amount):
        view = buffer.at[pl.ds(0, amount)]
        pltpu.make_async_copy(view, view, sems.at[kind]).wait()

    row_of = lax.rem(iota((8, rows), 1), clus_here) == iota((8, rows), 0)
    diag_of = iota((quarter, LANES), 0) == iota((quarter, LANES), 1)
    below = iota((half, LANES), 1) < iota((half, LANES), 0)
    lane1 = iota((1, LANES), 1)
    lane8 = iota((8, LANES), 1)
    sub8 = iota((8, LANES), 0)

    place = iota((rows // 16, 16, LANES), 1) // 4

    def tiles_of(s):
        groups = xbuf[s].reshape(rows // 16, 48, LANES)
        first, second, third = groups[:, :16], groups[:, 16:32], groups[:, 32:]
        a = jnp.where(place == 2, second, jnp.where(place == 1, third, first))
        b = jnp.where(place == 1, first, jnp.where(place == 2, third, second))
        c = jnp.where(place == 2, first, jnp.where(place == 1, second, third))
        b = jnp.concatenate([b[:, 4:], b[:, :4]], axis=1)
        c = jnp.concatenate([c[:, 8:], c[:, :8]], axis=1)
        return [tile.reshape(rows, LANES) for tile in (a, b, c)]

    chances = jnp.zeros((1, LANES), F32)
    groups = jnp.zeros((1, LANES), F32)
    group_rows = jnp.zeros((n_clus, LANES), jnp.int32)
    sub_n = iota((n_clus, LANES), 0)
    for i in range(n_clus):
        chances = jnp.where(lane1 == i, prob_ref[i], chances)
        groups = jnp.where(lane1 == i, branch_ref[i].astype(F32), groups)
        group_rows = jnp.where(sub_n == i, branch_ref[i], group_rows)
        chance[my_base + i] = jnp.where(sub8 == branch_ref[i], prob_ref[i], 0.0)
    send_t[0:1, :] = chances
    send_t[1:2, :] = groups
    t_copy = remote(send_t, recv_t, 2, (other * inner + my_inner, me))

    def local(k, carry):
        s = lax.rem(me + 1 + k, n_clus)
        x_copy(s).wait()
        a, b, c = tiles_of(s)
        cost_even, cost_odd = costs(s)
        part_even = dot_nt(
            jnp.concatenate([lhs_even[...], cost_even], axis=0), jnp.concatenate([a, b], axis=1)
        )
        part_odd = dot_nt(
            jnp.concatenate([lhs_odd[...], cost_odd], axis=0), jnp.concatenate([b, c], axis=1)
        )
        pushed_even = jnp.sum(
            jnp.where(row_of, part_even[quarter : quarter + 8], 0.0), axis=0, keepdims=True
        )
        pushed_odd = jnp.sum(
            jnp.where(row_of, part_odd[quarter : quarter + 8], 0.0), axis=0, keepdims=True
        )
        pushed = jnp.concatenate([pushed_even, pushed_odd], axis=1)
        push_buf[s] = pushed
        paired = jnp.concatenate([part_even[:quarter], part_odd[:quarter]], axis=1).astype(BF16)
        pt_buf[s] = paired
        pushed_rows = jnp.broadcast_to(pushed, (16, 2 * rows)).astype(BF16)
        left = jnp.concatenate([paired, pushed_rows], axis=0)
        right = jnp.concatenate([left, jnp.zeros((16, 2 * rows), BF16)], axis=0)
        product = dot_nt(left, right)
        schur = product[:quarter]
        low = pltpu.roll(schur[half:], LANES - half, 1)
        send_m[s] = jnp.where(below, low, schur[:half]).astype(BF16)
        send_v[s, 0:1, :] = product[quarter : quarter + 1]
        send_v[s, 1:2, :] = jnp.sum(jnp.where(diag_of, schur, 0.0), axis=0, keepdims=True)

        @pl.when(k == 0)
        def _():
            pl.semaphore_wait(barrier, plane - 1 + inner - 1)
            t_copy.start()

        @pl.when(k < scen_here - 1)
        def _():
            remote(send_m.at[s], recv_m.at[me], 0, (g, s)).start()
            remote(send_v.at[s], recv_v.at[me], 1, (g, s)).start()

        return carry

    lax.fori_loop(0, scen_here, local, 0)

    table[...] = jnp.zeros((8, LANES), F32)
    table[:, 0:split_at] = jnp.broadcast_to(root_ref[...], (8, split_at))
    table[:, split_at:quarter] = bprev_ref[...]
    branch = branch_ref[me]
    anchor = jnp.sum(jnp.where(sub8 == branch, table[...], 0.0), axis=0, keepdims=True)
    mult = jnp.concatenate(
        [mult_ref[pl.ds(me, 1), :], jnp.zeros((1, LANES - quarter), F32)], axis=1
    )
    t_copy.wait_recv()
    far_chance = recv_t[0:1, :]
    far_group = recv_t[1:2, :]
    for i in range(n_clus):
        member = sub8.astype(F32) == far_group[:, i : i + 1]
        chance[other * n_clus + i] = jnp.where(member, far_chance[:, i : i + 1], 0.0)
    mass = chance[0]
    for i in range(1, plane):
        mass = mass + chance[i]
    inv_mass = jnp.where(mass > 0.0, 1.0 / jnp.where(mass > 0.0, mass, 1.0), 0.0)

    recv_m[me] = send_m[me]
    recv_v[me] = send_v[me]
    await_all(recv_m, 0, recv_sem, n_clus - 1)
    await_all(recv_v, 1, recv_sem, n_clus - 1)
    mats = [recv_m[j].astype(F32) for j in range(n_clus)]
    vecs = [recv_v[j] for j in range(n_clus)]
    while len(mats) > 1:
        mats = [mats[i] + mats[i + 1] for i in range(0, len(mats), 2)]
        vecs = [vecs[i] + vecs[i + 1] for i in range(0, len(vecs), 2)]
    mat, vec = mats[0], vecs[0]

    lane_h = iota((half, LANES), 1)
    row_h = iota((half, LANES), 0)
    flipped = jnp.concatenate([mat, jnp.zeros((LANES - half, LANES), F32)], axis=0).T
    flip_a = flipped[:half]
    top = jnp.where(lane_h > row_h, mat, flip_a)
    low = jnp.where(lane_h < row_h, mat, flip_a)
    low = pltpu.roll(low, half, 1)
    bottom = jnp.where(lane_h < half, flipped[half:quarter], low)
    schur = jnp.concatenate([top, bottom], axis=0)
    lane_q = iota((quarter, LANES), 1)
    schur = jnp.where(diag_of, vec[1:2], schur)
    system = jnp.where(diag_of, 1.0 + penalty * schur, penalty * schur)
    system = jnp.where(lane_q < quarter, system, 0.0)
    side = jnp.where(lane1 < quarter, mult - penalty * (vec[0:1] + anchor), 0.0)
    side_rows = jnp.where(sub8 == 0, side, 0.0)
    solved = eliminate(jnp.concatenate([system, side_rows], axis=0), quarter)
    prices = solved[quarter : quarter + 1]
    bid = anchor + (prices - mult) / penalty
    msg[0:1, :] = prices
    msg[1:2, :] = jnp.where(lane1 < quarter, bid, jnp.where(lane1 == quarter, 1.0, 0.0))
    recv_p[my_slot] = msg[...]

    def send_p(j, carry):
        slot = lax.rem(my_slot + j, plane)
        remote(msg, recv_p.at[my_slot], 3, plane_device(slot)).start()
        return carry

    lax.fori_loop(1, plane, send_p, 0, unroll=True)
    await_all(recv_p, 3, recv_sem, plane - 1)

    def bid_tile(i):
        return jnp.broadcast_to(recv_p[i, 1:2, :], (8, LANES))

    totals = [chance[i] * bid_tile(i) for i in range(plane)]
    while len(totals) > 1:
        totals = [totals[i] + totals[i + 1] for i in range(0, len(totals), 2)]
    mean = totals[0] * inv_mass
    squares = []
    for i in range(plane):
        away = bid_tile(i) - mean
        squares.append(chance[i] * (away * away))
    while len(squares) > 1:
        squares = [squares[i] + squares[i + 1] for i in range(0, len(squares), 2)]
    square = jnp.sum(jnp.where(lane8 < quarter, squares[0], 0.0), axis=0, keepdims=True)
    square = jnp.sum(square, axis=1, keepdims=True)
    stat[...] = jnp.where(
        lane8 < quarter, mean, jnp.where(lane8 == quarter, mass, jnp.where(sub8 == 0, square, 0.0))
    )
    recv_s[my_inner] = stat[...]

    def send_s(j, carry):
        slot = lax.rem(my_inner + j, inner)
        remote(stat, recv_s.at[my_inner], 4, line_device(slot)).start()
        return carry

    lax.fori_loop(1, inner, send_s, 0, unroll=True)

    def powers(s, carry):
        price = recv_p[my_base + s, 0:1, :][:, :quarter]
        price = jnp.broadcast_to(price, (16, quarter)).astype(BF16)
        step = jnp.dot(price, pt_buf[s], preferred_element_type=F32)
        moved = push_buf[s] + step[0:1]
        stacked = jnp.concatenate(
            [
                jnp.where(row_of, moved[:, :rows], 0.0)[:clus_here],
                jnp.where(row_of, moved[:, rows:], 0.0)[:clus_here],
                jnp.zeros((16 - 2 * clus_here, rows), F32),
            ],
            axis=0,
        ).astype(BF16)
        out = jnp.dot(stacked, jnp.concatenate(tiles_of(s), axis=1), preferred_element_type=F32)
        from_odd = pltpu.roll(out[clus_here : 2 * clus_here, LANES:], LANES + LANES // 2, 1)
        total = out[:clus_here, : 2 * LANES] + from_odd
        power_ref[s] = -total[:, :width]
        return carry

    lax.fori_loop(0, scen_here, powers, 0, unroll=2)
    mine = recv_p[pl.ds(my_base, n_clus), 1, :]
    bid_ref[...] = mine[:, :quarter]
    await_all(send_m, 0, send_sem, n_clus - 1)
    await_all(send_v, 1, send_sem, n_clus - 1)
    t_copy.wait_send()
    await_all(recv_p, 3, send_sem, plane - 1)

    await_all(recv_s, 4, recv_sem, inner - 1)
    parts = [recv_s[j] for j in range(inner)]
    weights = [jnp.broadcast_to(part[:, quarter : quarter + 1], (8, LANES)) for part in parts]
    sums = [part * weight for part, weight in zip(parts, weights)]
    heavy = list(weights)
    while len(sums) > 1:
        sums = [sums[i] + sums[i + 1] for i in range(0, len(sums), 2)]
        heavy = [heavy[i] + heavy[i + 1] for i in range(0, len(heavy), 2)]
    whole = jnp.sum(sums[0], axis=0, keepdims=True)
    whole_mass = jnp.sum(heavy[0], axis=0, keepdims=True)
    node = jnp.where(lane8 < split_at, whole / whole_mass, sums[0] / heavy[0])
    mean_ref[...] = node[:, :quarter]
    target = jnp.zeros((n_clus, LANES), F32)
    for b in range(branch_count):
        target = jnp.where(group_rows == b, node[b : b + 1], target)
    next_ref[...] = mult_ref[...] + penalty * (mine - target)[:, :quarter]
    spread = []
    within = []
    for part, weight in zip(parts, weights):
        away = part - node
        spread.append(weight * (away * away))
        within.append(part[0:1])
    while len(spread) > 1:
        spread = [spread[i] + spread[i + 1] for i in range(0, len(spread), 2)]
        within = [within[i] + within[i + 1] for i in range(0, len(within), 2)]
    both = jnp.sum(jnp.where(lane8 < quarter, spread[0], 0.0), axis=0, keepdims=True)
    both = both + jnp.where(lane1 == quarter + 1, within[0], 0.0)
    gap_ref[...] = jnp.sum(both, axis=1, keepdims=True) / (quarter * whole_mass[:, 0:1])
    await_all(recv_s, 4, send_sem, inner - 1)


def hand_out(*refs):
    count = len(refs) // 2
    for source, target in zip(refs[:count], refs[count:]):
        target[...] = source[...]


def solution(mesh):
    n_scen, n_clus = mesh.shape["scen"], mesh.shape["clus"]

    def step(
        factors,
        linear,
        arrival,
        departure,
        ev_count,
        prob,
        branch_of,
        multiplier,
        root_prev,
        branch_prev,
    ):
        scen_here, clus_here = factors.shape[:2]
        width = linear.shape[2]
        quarter = multiplier.shape[1]
        split_at = root_prev.shape[0]
        branch_count = branch_prev.shape[0]
        rows = quarter * clus_here
        plane = HALVES * n_clus
        inner = n_scen // HALVES
        tiles = factors.reshape(scen_here, clus_here, 3 * quarter, LANES)
        tiles = tiles.transpose(0, 2, 1, 3).reshape(scen_here, 3 * rows, LANES)
        vmem = pl.BlockSpec(memory_space=pltpu.VMEM)
        dma = pltpu.SemaphoreType.DMA
        shapes = (
            jax.ShapeDtypeStruct((scen_here, clus_here, width), F32),
            jax.ShapeDtypeStruct((scen_here, quarter), F32),
            jax.ShapeDtypeStruct((scen_here, quarter), F32),
            jax.ShapeDtypeStruct((branch_count, quarter), F32),
            jax.ShapeDtypeStruct((1, 1), F32),
        )
        results = pl.pallas_call(
            functools.partial(
                kernel, n_scen, n_clus, clus_here, quarter, split_at, branch_count
            ),
            out_shape=shapes,
            in_specs=[pl.BlockSpec(memory_space=pl.ANY)] * 10,
            out_specs=(vmem,) * 5,
            scratch_shapes=[
                pltpu.VMEM((scen_here, 3 * rows, LANES), BF16),
                pltpu.VMEM(linear.shape, F32),
                pltpu.SMEM((clus_here, scen_here), jnp.int32),
                pltpu.SMEM((clus_here, scen_here), jnp.int32),
                pltpu.SMEM((clus_here,), jnp.int32),
                pltpu.SMEM((scen_here,), F32),
                pltpu.SMEM((scen_here,), jnp.int32),
                pltpu.VMEM(multiplier.shape, F32),
                pltpu.VMEM((1, split_at), F32),
                pltpu.VMEM(branch_prev.shape, F32),
                pltpu.VMEM((scen_here, quarter, 2 * rows), BF16),
                pltpu.VMEM((scen_here, 1, 2 * rows), F32),
                pltpu.VMEM((quarter, 2 * LANES), BF16),
                pltpu.VMEM((quarter, 2 * LANES), BF16),
                pltpu.VMEM((8, LANES), F32),
                pltpu.VMEM((plane, 8, LANES), F32),
                pltpu.VMEM((n_clus, quarter // 2, LANES), BF16),
                pltpu.VMEM((n_clus, 2, LANES), F32),
                pltpu.VMEM((n_clus, quarter // 2, LANES), BF16),
                pltpu.VMEM((n_clus, 2, LANES), F32),
                pltpu.VMEM((2, LANES), F32),
                pltpu.VMEM((2, LANES), F32),
                pltpu.VMEM((2, LANES), F32),
                pltpu.VMEM((plane, 2, LANES), F32),
                pltpu.VMEM((8, LANES), F32),
                pltpu.VMEM((inner, 8, LANES), F32),
                dma((9,)),
                dma((scen_here,)),
                dma((5,)),
                dma((5,)),
            ],
            compiler_params=pltpu.CompilerParams(collective_id=0, has_side_effects=True),
        )(
            tiles,
            linear,
            arrival.T,
            departure.T,
            ev_count,
            prob,
            branch_of,
            multiplier,
            root_prev[None, :],
            branch_prev,
        )
        power, bid, following, mean, gap = pl.pallas_call(
            hand_out, out_shape=shapes, in_specs=[vmem] * 5, out_specs=(vmem,) * 5
        )(*results)
        return (power, bid, following, mean, gap.reshape(()))

    return jax.shard_map(
        step,
        mesh=mesh,
        in_specs=(
            P("scen", "clus", None),
            P("scen", "clus", None),
            P("scen", "clus"),
            P("scen", "clus"),
            P("clus"),
            P("scen"),
            P("scen"),
            P("scen", None),
            P(),
            P(),
        ),
        out_specs=(P("scen", "clus", None), P("scen", None), P("scen", None), P(), P()),
        check_vma=False,
    )
```

```python
import functools

import jax
import jax.numpy as jnp
from jax import lax
from jax.experimental import pallas as pl
from jax.experimental.pallas import tpu as pltpu
from jax.sharding import PartitionSpec as P

MESH = pl.DeviceIdType.MESH
HALVES = 2
LANES = 128
F32 = jnp.float32
BF16 = jnp.bfloat16


def iota(shape, axis):
    return lax.broadcasted_iota(jnp.int32, shape, axis)


def dot_nt(a, b):
    return lax.dot_general(a, b, (((1,), (1,)), ((), ())), preferred_element_type=F32)


def spread_row(tile, p):
    return jnp.broadcast_to(tile[p : p + 1, :], (8, LANES))


def sweep(matrix, first, count, trips):
    height = matrix.shape[0]
    lane = iota((8, LANES), 1)
    sub = iota((8, LANES), 0)
    lane_all = iota((height, LANES), 1)

    def trip(k, matrix):
        base = first + 8 * k
        columns = [
            jnp.take_along_axis(matrix, jnp.full((height, LANES), base + q, jnp.int32), axis=1)
            for q in range(8)
        ]
        block = matrix[:8]
        own = [column[:8] for column in columns]
        for p in range(8):
            here = sub == p
            inv = 1.0 / spread_row(own[p], p)
            factor = jnp.where(here, 0.0, own[p])
            for q in range(p + 1, 8):
                scaled = spread_row(own[q], p) * inv
                own[q] = jnp.where(here, scaled, own[q] - factor * scaled)
            scaled = spread_row(block, p) * inv
            block = jnp.where(here, scaled, block - factor * scaled)
            block = jnp.where(lane == base + p, jnp.where(here, inv, -own[p] * inv), block)
        weight = jnp.where((lane >= base) & (lane < base + 8), -block, block)
        taken = (lane_all >= base) & (lane_all < base + 8)
        terms = [
            columns[q] * jnp.broadcast_to(weight[q : q + 1, :], (height, LANES)) for q in range(8)
        ]
        while len(terms) > 1:
            terms = [terms[i] + terms[i + 1] for i in range(0, len(terms), 2)]
        matrix = jnp.where(taken, 0.0, matrix) - terms[0]
        return jnp.concatenate([matrix[8:count], matrix[:8], matrix[count:]], axis=0)

    return lax.fori_loop(0, trips, trip, matrix)


def solve_row(system, side_rows, quarter):
    half = quarter // 2
    matrix = jnp.concatenate([system, side_rows], axis=0)
    matrix = sweep(matrix, 0, quarter, half // 8)
    matrix = jnp.concatenate([matrix[:half], matrix[quarter:]], axis=0)
    matrix = sweep(matrix, half, half, half // 8)
    return matrix[half : half + 1]


def kernel(
    n_scen,
    n_clus,
    clus_here,
    quarter,
    split_at,
    branch_count,
    x_hbm,
    lin_hbm,
    arr_hbm,
    dep_hbm,
    ev_hbm,
    prob_hbm,
    branch_hbm,
    mult_hbm,
    root_hbm,
    bprev_hbm,
    power_ref,
    bid_ref,
    next_ref,
    mean_ref,
    gap_ref,
    xbuf,
    lin_ref,
    arr_ref,
    dep_ref,
    ev_ref,
    prob_ref,
    branch_ref,
    mult_ref,
    root_ref,
    bprev_ref,
    pt_buf,
    push_buf,
    lhs_even,
    lhs_odd,
    table,
    chance,
    send_m,
    send_v,
    recv_m,
    recv_v,
    send_t,
    recv_t,
    msg,
    recv_p,
    stat,
    recv_s,
    small_sem,
    x_sem,
    send_sem,
    recv_sem,
):
    scen_here = n_clus
    half = quarter // 2
    width = 2 * quarter
    rows = quarter * clus_here
    inner = n_scen // HALVES
    plane = HALVES * n_clus
    penalty = 1.0 / (clus_here * n_clus)
    g = lax.axis_index("scen")
    me = lax.axis_index("clus")
    my_half = g // inner
    my_inner = lax.rem(g, inner)
    my_slot = my_half * n_clus + me
    my_base = my_half * n_clus
    other = 1 - my_half

    barrier = pltpu.get_barrier_semaphore()

    def plane_device(slot):
        return ((slot // n_clus) * inner + my_inner, lax.rem(slot, n_clus))

    def line_device(slot):
        return (my_half * inner + slot, me)

    def greet_plane(j, carry):
        pl.semaphore_signal(
            barrier, inc=1, device_id=plane_device(lax.rem(my_slot + j, plane)), device_id_type=MESH
        )
        return carry

    def greet_line(j, carry):
        pl.semaphore_signal(
            barrier, inc=1, device_id=line_device(lax.rem(my_inner + j, inner)), device_id_type=MESH
        )
        return carry

    small = [
        pltpu.make_async_copy(source, target, small_sem.at[i])
        for i, (source, target) in enumerate(
            (
                (lin_hbm, lin_ref),
                (arr_hbm, arr_ref),
                (dep_hbm, dep_ref),
                (ev_hbm, ev_ref),
                (prob_hbm, prob_ref),
                (branch_hbm, branch_ref),
                (mult_hbm, mult_ref),
                (root_hbm, root_ref),
                (bprev_hbm, bprev_ref),
            )
        )
    ]
    for copy in small:
        copy.start()

    def x_copy(s):
        return pltpu.make_async_copy(x_hbm.at[s], xbuf.at[s], x_sem.at[s])

    def start_x(k, carry):
        x_copy(lax.rem(me + 1 + k, n_clus)).start()
        return carry

    lax.fori_loop(0, scen_here, start_x, 0)
    lax.fori_loop(1, plane, greet_plane, 0)
    lax.fori_loop(1, inner, greet_line, 0)

    t_index = iota((quarter, 2 * LANES), 0)
    l_index = iota((quarter, 2 * LANES), 1)
    even = jnp.where(l_index == t_index, 1.0, 0.0) - jnp.where(l_index == t_index + quarter, 1.0, 0.0)
    shifted = t_index + LANES // 2
    odd = jnp.where(l_index == shifted, 1.0, 0.0) - jnp.where(l_index == shifted + quarter, 1.0, 0.0)
    lhs_even[...] = even.astype(BF16)
    lhs_odd[...] = odd.astype(BF16)

    for copy in small:
        copy.wait()

    lane2 = iota((8, 2 * LANES), 1)
    hour = jnp.where(lane2 < quarter, lane2, lane2 - quarter)
    sub2 = iota((8, 2 * LANES), 0)
    count = jnp.zeros((8, 2 * LANES), F32)
    for c in range(clus_here):
        count = jnp.where(sub2 == c, ev_ref[c].astype(F32) / 16.0, count)

    def costs(s):
        first = jnp.zeros((8, 2 * LANES), jnp.int32)
        last = jnp.zeros((8, 2 * LANES), jnp.int32)
        for c in range(clus_here):
            first = jnp.where(sub2 == c, arr_ref[c, s], first)
            last = jnp.where(sub2 == c, dep_ref[c, s], last)
        inside = jnp.where((hour >= first) & (hour < last), 1.0, 0.0)
        cost = jnp.concatenate(
            [lin_ref[s], jnp.zeros((clus_here, 2 * LANES - width), F32)], axis=1
        )
        cost = jnp.concatenate([cost, jnp.zeros((8 - clus_here, 2 * LANES), F32)], axis=0)
        value = cost * (inside * count)
        turned = pltpu.roll(value, LANES // 2, 1)
        pad = jnp.zeros((8, 2 * LANES), F32)
        return (
            jnp.concatenate([value, pad], axis=0).astype(BF16),
            jnp.concatenate([turned, pad], axis=0).astype(BF16),
        )

    def remote(source, target, kind, device):
        return pltpu.make_async_remote_copy(
            src_ref=source,
            dst_ref=target,
            send_sem=send_sem.at[kind],
            recv_sem=recv_sem.at[kind],
            device_id=device,
            device_id_type=MESH,
        )

    def await_all(buffer, kind, sems, amount):
        view = buffer.at[pl.ds(0, amount)]
        pltpu.make_async_copy(view, view, sems.at[kind]).wait()

    row_of = lax.rem(iota((8, rows), 1), clus_here) == iota((8, rows), 0)
    diag_of = iota((quarter, LANES), 0) == iota((quarter, LANES), 1)
    below = iota((half, LANES), 1) < iota((half, LANES), 0)
    lane1 = iota((1, LANES), 1)
    lane8 = iota((8, LANES), 1)
    sub8 = iota((8, LANES), 0)

    place = iota((rows // 16, 16, LANES), 1) // 4

    def tiles_of(s):
        groups = xbuf[s].reshape(rows // 16, 48, LANES)
        first, second, third = groups[:, :16], groups[:, 16:32], groups[:, 32:]
        a = jnp.where(place == 2, second, jnp.where(place == 1, third, first))
        b = jnp.where(place == 1, first, jnp.where(place == 2, third, second))
        c = jnp.where(place == 2, first, jnp.where(place == 1, second, third))
        b = jnp.concatenate([b[:, 4:], b[:, :4]], axis=1)
        c = jnp.concatenate([c[:, 8:], c[:, :8]], axis=1)
        return [tile.reshape(rows, LANES) for tile in (a, b, c)]

    chances = jnp.zeros((1, LANES), F32)
    groups = jnp.zeros((1, LANES), F32)
    group_rows = jnp.zeros((n_clus, LANES), jnp.int32)
    sub_n = iota((n_clus, LANES), 0)
    for i in range(n_clus):
        chances = jnp.where(lane1 == i, prob_ref[i], chances)
        groups = jnp.where(lane1 == i, branch_ref[i].astype(F32), groups)
        group_rows = jnp.where(sub_n == i, branch_ref[i], group_rows)
        chance[my_base + i] = jnp.where(sub8 == branch_ref[i], prob_ref[i], 0.0)
    send_t[0:1, :] = chances
    send_t[1:2, :] = groups
    t_copy = remote(send_t, recv_t, 2, (other * inner + my_inner, me))

    def local(k, carry):
        s = lax.rem(me + 1 + k, n_clus)
        x_copy(s).wait()
        a, b, c = tiles_of(s)
        cost_even, cost_odd = costs(s)
        part_even = dot_nt(
            jnp.concatenate([lhs_even[...], cost_even], axis=0), jnp.concatenate([a, b], axis=1)
        )
        part_odd = dot_nt(
            jnp.concatenate([lhs_odd[...], cost_odd], axis=0), jnp.concatenate([b, c], axis=1)
        )
        pushed_even = jnp.sum(
            jnp.where(row_of, part_even[quarter : quarter + 8], 0.0), axis=0, keepdims=True
        )
        pushed_odd = jnp.sum(
            jnp.where(row_of, part_odd[quarter : quarter + 8], 0.0), axis=0, keepdims=True
        )
        pushed = jnp.concatenate([pushed_even, pushed_odd], axis=1)
        push_buf[s] = pushed
        paired = jnp.concatenate([part_even[:quarter], part_odd[:quarter]], axis=1).astype(BF16)
        pt_buf[s] = paired
        pushed_rows = jnp.broadcast_to(pushed, (16, 2 * rows)).astype(BF16)
        left = jnp.concatenate([paired, pushed_rows], axis=0)
        product = dot_nt(left, paired)
        product = jnp.concatenate([product, jnp.zeros((quarter + 16, LANES - quarter), F32)], axis=1)
        schur = product[:quarter]
        low = pltpu.roll(schur[half:], LANES - half, 1)
        send_m[s] = jnp.where(below, low, schur[:half]).astype(BF16)
        send_v[s, 0:1, :] = product[quarter : quarter + 1]
        send_v[s, 1:2, :] = jnp.sum(jnp.where(diag_of, schur, 0.0), axis=0, keepdims=True)

        @pl.when(k == 0)
        def _():
            pl.semaphore_wait(barrier, plane - 1 + inner - 1)
            t_copy.start()

        @pl.when(k < scen_here - 1)
        def _():
            remote(send_m.at[s], recv_m.at[me], 0, (g, s)).start()
            remote(send_v.at[s], recv_v.at[me], 1, (g, s)).start()

        return carry

    lax.fori_loop(0, scen_here, local, 0)

    table[...] = jnp.zeros((8, LANES), F32)
    table[:, 0:split_at] = jnp.broadcast_to(root_ref[...], (8, split_at))
    table[:, split_at:quarter] = bprev_ref[...]
    branch = branch_ref[me]
    anchor = jnp.sum(jnp.where(sub8 == branch, table[...], 0.0), axis=0, keepdims=True)
    mult = jnp.concatenate(
        [mult_ref[pl.ds(me, 1), :], jnp.zeros((1, LANES - quarter), F32)], axis=1
    )
    t_copy.wait_recv()
    far_chance = recv_t[0:1, :]
    far_group = recv_t[1:2, :]
    for i in range(n_clus):
        member = sub8.astype(F32) == far_group[:, i : i + 1]
        chance[other * n_clus + i] = jnp.where(member, far_chance[:, i : i + 1], 0.0)
    mass = chance[0]
    for i in range(1, plane):
        mass = mass + chance[i]
    inv_mass = jnp.where(mass > 0.0, 1.0 / jnp.where(mass > 0.0, mass, 1.0), 0.0)

    recv_m[me] = send_m[me]
    recv_v[me] = send_v[me]
    await_all(recv_m, 0, recv_sem, n_clus - 1)
    await_all(recv_v, 1, recv_sem, n_clus - 1)
    mats = [recv_m[j].astype(F32) for j in range(n_clus)]
    vecs = [recv_v[j] for j in range(n_clus)]
    while len(mats) > 1:
        mats = [mats[i] + mats[i + 1] for i in range(0, len(mats), 2)]
        vecs = [vecs[i] + vecs[i + 1] for i in range(0, len(vecs), 2)]
    mat, vec = mats[0], vecs[0]

    lane_h = iota((half, LANES), 1)
    row_h = iota((half, LANES), 0)
    flipped = jnp.concatenate([mat, jnp.zeros((LANES - half, LANES), F32)], axis=0).T
    flip_a = flipped[:half]
    top = jnp.where(lane_h > row_h, mat, flip_a)
    low = jnp.where(lane_h < row_h, mat, flip_a)
    low = pltpu.roll(low, half, 1)
    bottom = jnp.where(lane_h < half, flipped[half:quarter], low)
    schur = jnp.concatenate([top, bottom], axis=0)
    lane_q = iota((quarter, LANES), 1)
    schur = jnp.where(diag_of, vec[1:2], schur)
    system = jnp.where(diag_of, 1.0 + penalty * schur, penalty * schur)
    system = jnp.where(lane_q < quarter, system, 0.0)
    side = jnp.where(lane1 < quarter, mult - penalty * (vec[0:1] + anchor), 0.0)
    side_rows = jnp.where(sub8 == 0, side, 0.0)
    prices = solve_row(system, side_rows, quarter)
    bid = anchor + (prices - mult) / penalty
    msg[0:1, :] = prices
    msg[1:2, :] = jnp.where(lane1 < quarter, bid, jnp.where(lane1 == quarter, 1.0, 0.0))
    recv_p[my_slot] = msg[...]

    def send_p(j, carry):
        slot = lax.rem(my_slot + j, plane)
        remote(msg, recv_p.at[my_slot], 3, plane_device(slot)).start()
        return carry

    lax.fori_loop(1, plane, send_p, 0, unroll=True)
    await_all(recv_p, 3, recv_sem, plane - 1)

    def bid_tile(i):
        return jnp.broadcast_to(recv_p[i, 1:2, :], (8, LANES))

    totals = [chance[i] * bid_tile(i) for i in range(plane)]
    while len(totals) > 1:
        totals = [totals[i] + totals[i + 1] for i in range(0, len(totals), 2)]
    mean = totals[0] * inv_mass
    squares = []
    for i in range(plane):
        away = bid_tile(i) - mean
        squares.append(chance[i] * (away * away))
    while len(squares) > 1:
        squares = [squares[i] + squares[i + 1] for i in range(0, len(squares), 2)]
    square = jnp.sum(jnp.where(lane8 < quarter, squares[0], 0.0), axis=0, keepdims=True)
    square = jnp.sum(square, axis=1, keepdims=True)
    stat[...] = jnp.where(
        lane8 < quarter, mean, jnp.where(lane8 == quarter, mass, jnp.where(sub8 == 0, square, 0.0))
    )
    recv_s[my_inner] = stat[...]

    def send_s(j, carry):
        slot = lax.rem(my_inner + j, inner)
        remote(stat, recv_s.at[my_inner], 4, line_device(slot)).start()
        return carry

    lax.fori_loop(1, inner, send_s, 0, unroll=True)

    def powers(s, carry):
        price = recv_p[my_base + s, 0:1, :][:, :quarter]
        price = jnp.broadcast_to(price, (16, quarter)).astype(BF16)
        step = jnp.dot(price, pt_buf[s], preferred_element_type=F32)
        moved = push_buf[s] + step[0:1]
        stacked = jnp.concatenate(
            [
                jnp.where(row_of, moved[:, :rows], 0.0)[:clus_here],
                jnp.where(row_of, moved[:, rows:], 0.0)[:clus_here],
                jnp.zeros((16 - 2 * clus_here, rows), F32),
            ],
            axis=0,
        ).astype(BF16)
        out = jnp.dot(stacked, jnp.concatenate(tiles_of(s), axis=1), preferred_element_type=F32)
        from_odd = pltpu.roll(out[clus_here : 2 * clus_here, LANES:], LANES + LANES // 2, 1)
        total = out[:clus_here, : 2 * LANES] + from_odd
        power_ref[s] = -total[:, :width]
        return carry

    lax.fori_loop(0, scen_here, powers, 0, unroll=2)
    mine = recv_p[pl.ds(my_base, n_clus), 1, :]
    bid_ref[...] = mine[:, :quarter]
    await_all(send_m, 0, send_sem, n_clus - 1)
    await_all(send_v, 1, send_sem, n_clus - 1)
    t_copy.wait_send()
    await_all(recv_p, 3, send_sem, plane - 1)

    await_all(recv_s, 4, recv_sem, inner - 1)
    parts = [recv_s[j] for j in range(inner)]
    weights = [jnp.broadcast_to(part[:, quarter : quarter + 1], (8, LANES)) for part in parts]
    sums = [part * weight for part, weight in zip(parts, weights)]
    heavy = list(weights)
    while len(sums) > 1:
        sums = [sums[i] + sums[i + 1] for i in range(0, len(sums), 2)]
        heavy = [heavy[i] + heavy[i + 1] for i in range(0, len(heavy), 2)]
    whole = jnp.sum(sums[0], axis=0, keepdims=True)
    whole_mass = jnp.sum(heavy[0], axis=0, keepdims=True)
    node = jnp.where(lane8 < split_at, whole / whole_mass, sums[0] / heavy[0])
    mean_ref[...] = node[:, :quarter]
    target = jnp.zeros((n_clus, LANES), F32)
    for b in range(branch_count):
        target = jnp.where(group_rows == b, node[b : b + 1], target)
    next_ref[...] = mult_ref[...] + penalty * (mine - target)[:, :quarter]
    spread = []
    within = []
    for part, weight in zip(parts, weights):
        away = part - node
        spread.append(weight * (away * away))
        within.append(part[0:1])
    while len(spread) > 1:
        spread = [spread[i] + spread[i + 1] for i in range(0, len(spread), 2)]
        within = [within[i] + within[i + 1] for i in range(0, len(within), 2)]
    both = jnp.sum(jnp.where(lane8 < quarter, spread[0], 0.0), axis=0, keepdims=True)
    both = both + jnp.where(lane1 == quarter + 1, within[0], 0.0)
    gap_ref[...] = jnp.sum(both, axis=1, keepdims=True) / (quarter * whole_mass[:, 0:1])
    await_all(recv_s, 4, send_sem, inner - 1)


def hand_out(*refs):
    count = len(refs) // 2
    for source, target in zip(refs[:count], refs[count:]):
        target[...] = source[...]


def solution(mesh):
    n_scen, n_clus = mesh.shape["scen"], mesh.shape["clus"]

    def step(
        factors,
        linear,
        arrival,
        departure,
        ev_count,
        prob,
        branch_of,
        multiplier,
        root_prev,
        branch_prev,
    ):
        scen_here, clus_here = factors.shape[:2]
        width = linear.shape[2]
        quarter = multiplier.shape[1]
        split_at = root_prev.shape[0]
        branch_count = branch_prev.shape[0]
        rows = quarter * clus_here
        plane = HALVES * n_clus
        inner = n_scen // HALVES
        tiles = factors.reshape(scen_here, clus_here, 3 * quarter, LANES)
        tiles = tiles.transpose(0, 2, 1, 3).reshape(scen_here, 3 * rows, LANES)
        vmem = pl.BlockSpec(memory_space=pltpu.VMEM)
        dma = pltpu.SemaphoreType.DMA
        shapes = (
            jax.ShapeDtypeStruct((scen_here, clus_here, width), F32),
            jax.ShapeDtypeStruct((scen_here, quarter), F32),
            jax.ShapeDtypeStruct((scen_here, quarter), F32),
            jax.ShapeDtypeStruct((branch_count, quarter), F32),
            jax.ShapeDtypeStruct((1, 1), F32),
        )
        results = pl.pallas_call(
            functools.partial(
                kernel, n_scen, n_clus, clus_here, quarter, split_at, branch_count
            ),
            out_shape=tuple(pltpu.VMEM(shape.shape, shape.dtype) for shape in shapes),
            in_specs=[pl.BlockSpec(memory_space=pl.ANY)] * 10,
            out_specs=(vmem,) * 5,
            scratch_shapes=[
                pltpu.VMEM((scen_here, 3 * rows, LANES), BF16),
                pltpu.VMEM(linear.shape, F32),
                pltpu.SMEM((clus_here, scen_here), jnp.int32),
                pltpu.SMEM((clus_here, scen_here), jnp.int32),
                pltpu.SMEM((clus_here,), jnp.int32),
                pltpu.SMEM((scen_here,), F32),
                pltpu.SMEM((scen_here,), jnp.int32),
                pltpu.VMEM(multiplier.shape, F32),
                pltpu.VMEM((1, split_at), F32),
                pltpu.VMEM(branch_prev.shape, F32),
                pltpu.VMEM((scen_here, quarter, 2 * rows), BF16),
                pltpu.VMEM((scen_here, 1, 2 * rows), F32),
                pltpu.VMEM((quarter, 2 * LANES), BF16),
                pltpu.VMEM((quarter, 2 * LANES), BF16),
                pltpu.VMEM((8, LANES), F32),
                pltpu.VMEM((plane, 8, LANES), F32),
                pltpu.VMEM((n_clus, quarter // 2, LANES), BF16),
                pltpu.VMEM((n_clus, 2, LANES), F32),
                pltpu.VMEM((n_clus, quarter // 2, LANES), BF16),
                pltpu.VMEM((n_clus, 2, LANES), F32),
                pltpu.VMEM((2, LANES), F32),
                pltpu.VMEM((2, LANES), F32),
                pltpu.VMEM((2, LANES), F32),
                pltpu.VMEM((plane, 2, LANES), F32),
                pltpu.VMEM((8, LANES), F32),
                pltpu.VMEM((inner, 8, LANES), F32),
                dma((9,)),
                dma((scen_here,)),
                dma((5,)),
                dma((5,)),
            ],
            compiler_params=pltpu.CompilerParams(collective_id=0, has_side_effects=True),
        )(
            tiles,
            linear,
            arrival.T,
            departure.T,
            ev_count,
            prob,
            branch_of,
            multiplier,
            root_prev[None, :],
            branch_prev,
        )
        power, bid, following, mean, gap = pl.pallas_call(
            hand_out, out_shape=shapes, in_specs=[vmem] * 5, out_specs=(vmem,) * 5
        )(*[pltpu.with_memory_space_constraint(result, pltpu.VMEM) for result in results])
        return (power, bid, following, mean, gap.reshape(()))

    return jax.shard_map(
        step,
        mesh=mesh,
        in_specs=(
            P("scen", "clus", None),
            P("scen", "clus", None),
            P("scen", "clus"),
            P("scen", "clus"),
            P("clus"),
            P("scen"),
            P("scen"),
            P("scen", None),
            P(),
            P(),
        ),
        out_specs=(P("scen", "clus", None), P("scen", None), P("scen", None), P(), P()),
        check_vma=False,
    )
```

```python
import functools

import jax
import jax.numpy as jnp
from jax import lax
from jax.experimental import pallas as pl
from jax.experimental.pallas import tpu as pltpu
from jax.sharding import PartitionSpec as P

MESH = pl.DeviceIdType.MESH
HALVES = 2
LANES = 128
F32 = jnp.float32
BF16 = jnp.bfloat16


def iota(shape, axis):
    return lax.broadcasted_iota(jnp.int32, shape, axis)


def dot_nt(a, b):
    return lax.dot_general(a, b, (((1,), (1,)), ((), ())), preferred_element_type=F32)


def spread_row(tile, p):
    return jnp.broadcast_to(tile[p : p + 1, :], (8, LANES))


def sweep(matrix, first, count, trips):
    height = matrix.shape[0]
    lane = iota((8, LANES), 1)
    sub = iota((8, LANES), 0)
    lane_all = iota((height, LANES), 1)

    def trip(k, matrix):
        base = first + 8 * k
        columns = [
            jnp.take_along_axis(matrix, jnp.full((height, LANES), base + q, jnp.int32), axis=1)
            for q in range(8)
        ]
        block = matrix[:8]
        own = [column[:8] for column in columns]
        for p in range(8):
            here = sub == p
            inv = 1.0 / spread_row(own[p], p)
            factor = jnp.where(here, 0.0, own[p])
            for q in range(p + 1, 8):
                scaled = spread_row(own[q], p) * inv
                own[q] = jnp.where(here, scaled, own[q] - factor * scaled)
            scaled = spread_row(block, p) * inv
            block = jnp.where(here, scaled, block - factor * scaled)
            block = jnp.where(lane == base + p, jnp.where(here, inv, -own[p] * inv), block)
        weight = jnp.where((lane >= base) & (lane < base + 8), -block, block)
        taken = (lane_all >= base) & (lane_all < base + 8)
        terms = [
            columns[q] * jnp.broadcast_to(weight[q : q + 1, :], (height, LANES)) for q in range(8)
        ]
        while len(terms) > 1:
            terms = [terms[i] + terms[i + 1] for i in range(0, len(terms), 2)]
        matrix = jnp.where(taken, 0.0, matrix) - terms[0]
        return jnp.concatenate([matrix[8:count], matrix[:8], matrix[count:]], axis=0)

    return lax.fori_loop(0, trips, trip, matrix)


def solve_row(system, side_rows, quarter):
    half = quarter // 2
    matrix = jnp.concatenate([system, side_rows], axis=0)
    matrix = sweep(matrix, 0, quarter, half // 8)
    matrix = jnp.concatenate([matrix[:half], matrix[quarter:]], axis=0)
    matrix = sweep(matrix, half, half, half // 8)
    return matrix[half : half + 1]


def kernel(
    n_scen,
    n_clus,
    clus_here,
    quarter,
    split_at,
    branch_count,
    x_hbm,
    lin_hbm,
    arr_hbm,
    dep_hbm,
    ev_hbm,
    prob_hbm,
    branch_hbm,
    mult_hbm,
    root_hbm,
    bprev_hbm,
    power_ref,
    bid_ref,
    next_ref,
    mean_ref,
    gap_ref,
    xbuf,
    lin_ref,
    arr_ref,
    dep_ref,
    ev_ref,
    prob_ref,
    branch_ref,
    mult_ref,
    root_ref,
    bprev_ref,
    pt_buf,
    push_buf,
    lhs_even,
    lhs_odd,
    table,
    chance,
    send_m,
    send_v,
    recv_m,
    recv_v,
    send_t,
    recv_t,
    msg,
    recv_p,
    stat,
    recv_s,
    small_sem,
    x_sem,
    send_sem,
    recv_sem,
):
    scen_here = n_clus
    half = quarter // 2
    width = 2 * quarter
    rows = quarter * clus_here
    inner = n_scen // HALVES
    plane = HALVES * n_clus
    penalty = 1.0 / (clus_here * n_clus)
    g = lax.axis_index("scen")
    me = lax.axis_index("clus")
    my_half = g // inner
    my_inner = lax.rem(g, inner)
    my_slot = my_half * n_clus + me
    my_base = my_half * n_clus
    other = 1 - my_half

    barrier = pltpu.get_barrier_semaphore()

    def plane_device(slot):
        return ((slot // n_clus) * inner + my_inner, lax.rem(slot, n_clus))

    def line_device(slot):
        return (my_half * inner + slot, me)

    def greet_plane(j, carry):
        pl.semaphore_signal(
            barrier, inc=1, device_id=plane_device(lax.rem(my_slot + j, plane)), device_id_type=MESH
        )
        return carry

    def greet_line(j, carry):
        pl.semaphore_signal(
            barrier, inc=1, device_id=line_device(lax.rem(my_inner + j, inner)), device_id_type=MESH
        )
        return carry

    small = [
        pltpu.make_async_copy(source, target, small_sem.at[i])
        for i, (source, target) in enumerate(
            (
                (lin_hbm, lin_ref),
                (arr_hbm, arr_ref),
                (dep_hbm, dep_ref),
                (ev_hbm, ev_ref),
                (prob_hbm, prob_ref),
                (branch_hbm, branch_ref),
                (mult_hbm, mult_ref),
                (root_hbm, root_ref),
                (bprev_hbm, bprev_ref),
            )
        )
    ]
    for copy in small:
        copy.start()

    def x_copy(s):
        return pltpu.make_async_copy(x_hbm.at[s], xbuf.at[s], x_sem.at[s])

    def start_x(k, carry):
        x_copy(lax.rem(me + 1 + k, n_clus)).start()
        return carry

    lax.fori_loop(0, scen_here, start_x, 0)
    lax.fori_loop(1, plane, greet_plane, 0)
    lax.fori_loop(1, inner, greet_line, 0)

    t_index = iota((quarter, 2 * LANES), 0)
    l_index = iota((quarter, 2 * LANES), 1)
    even = jnp.where(l_index == t_index, 1.0, 0.0) - jnp.where(l_index == t_index + quarter, 1.0, 0.0)
    shifted = t_index + LANES // 2
    odd = jnp.where(l_index == shifted, 1.0, 0.0) - jnp.where(l_index == shifted + quarter, 1.0, 0.0)
    lhs_even[...] = even.astype(BF16)
    lhs_odd[...] = odd.astype(BF16)

    for copy in small:
        copy.wait()

    lane2 = iota((8, 2 * LANES), 1)
    hour = jnp.where(lane2 < quarter, lane2, lane2 - quarter)
    sub2 = iota((8, 2 * LANES), 0)
    count = jnp.zeros((8, 2 * LANES), F32)
    for c in range(clus_here):
        count = jnp.where(sub2 == c, ev_ref[c].astype(F32) / 16.0, count)

    def costs(s):
        first = jnp.zeros((8, 2 * LANES), jnp.int32)
        last = jnp.zeros((8, 2 * LANES), jnp.int32)
        for c in range(clus_here):
            first = jnp.where(sub2 == c, arr_ref[c, s], first)
            last = jnp.where(sub2 == c, dep_ref[c, s], last)
        inside = jnp.where((hour >= first) & (hour < last), 1.0, 0.0)
        cost = jnp.concatenate(
            [lin_ref[s], jnp.zeros((clus_here, 2 * LANES - width), F32)], axis=1
        )
        cost = jnp.concatenate([cost, jnp.zeros((8 - clus_here, 2 * LANES), F32)], axis=0)
        value = cost * (inside * count)
        turned = pltpu.roll(value, LANES // 2, 1)
        pad = jnp.zeros((8, 2 * LANES), F32)
        return (
            jnp.concatenate([value, pad], axis=0).astype(BF16),
            jnp.concatenate([turned, pad], axis=0).astype(BF16),
        )

    def remote(source, target, kind, device):
        return pltpu.make_async_remote_copy(
            src_ref=source,
            dst_ref=target,
            send_sem=send_sem.at[kind],
            recv_sem=recv_sem.at[kind],
            device_id=device,
            device_id_type=MESH,
        )

    def await_all(buffer, kind, sems, amount):
        view = buffer.at[pl.ds(0, amount)]
        pltpu.make_async_copy(view, view, sems.at[kind]).wait()

    row_of = lax.rem(iota((8, rows), 1), clus_here) == iota((8, rows), 0)
    diag_of = iota((quarter, LANES), 0) == iota((quarter, LANES), 1)
    below = iota((half, LANES), 1) < iota((half, LANES), 0)
    lane1 = iota((1, LANES), 1)
    lane8 = iota((8, LANES), 1)
    sub8 = iota((8, LANES), 0)

    place = iota((rows // 16, 16, LANES), 1) // 4

    def tiles_of(s):
        groups = xbuf[s].reshape(rows // 16, 48, LANES)
        first, second, third = groups[:, :16], groups[:, 16:32], groups[:, 32:]
        a = jnp.where(place == 2, second, jnp.where(place == 1, third, first))
        b = jnp.where(place == 1, first, jnp.where(place == 2, third, second))
        c = jnp.where(place == 2, first, jnp.where(place == 1, second, third))
        b = jnp.concatenate([b[:, 4:], b[:, :4]], axis=1)
        c = jnp.concatenate([c[:, 8:], c[:, :8]], axis=1)
        return [tile.reshape(rows, LANES) for tile in (a, b, c)]

    chances = jnp.zeros((1, LANES), F32)
    groups = jnp.zeros((1, LANES), F32)
    group_rows = jnp.zeros((n_clus, LANES), jnp.int32)
    sub_n = iota((n_clus, LANES), 0)
    for i in range(n_clus):
        chances = jnp.where(lane1 == i, prob_ref[i], chances)
        groups = jnp.where(lane1 == i, branch_ref[i].astype(F32), groups)
        group_rows = jnp.where(sub_n == i, branch_ref[i], group_rows)
        chance[my_base + i] = jnp.where(sub8 == branch_ref[i], prob_ref[i], 0.0)
    send_t[0:1, :] = chances
    send_t[1:2, :] = groups
    t_copy = remote(send_t, recv_t, 2, (other * inner + my_inner, me))

    def local(k, carry):
        s = lax.rem(me + 1 + k, n_clus)
        x_copy(s).wait()
        a, b, c = tiles_of(s)
        cost_even, cost_odd = costs(s)
        part_even = dot_nt(
            jnp.concatenate([lhs_even[...], cost_even], axis=0), jnp.concatenate([a, b], axis=1)
        )
        part_odd = dot_nt(
            jnp.concatenate([lhs_odd[...], cost_odd], axis=0), jnp.concatenate([b, c], axis=1)
        )
        pushed_even = jnp.sum(
            jnp.where(row_of, part_even[quarter : quarter + 8], 0.0), axis=0, keepdims=True
        )
        pushed_odd = jnp.sum(
            jnp.where(row_of, part_odd[quarter : quarter + 8], 0.0), axis=0, keepdims=True
        )
        pushed = jnp.concatenate([pushed_even, pushed_odd], axis=1)
        push_buf[s] = pushed
        paired = jnp.concatenate([part_even[:quarter], part_odd[:quarter]], axis=1).astype(BF16)
        pt_buf[s] = paired
        pushed_rows = jnp.broadcast_to(pushed, (16, 2 * rows)).astype(BF16)
        left = jnp.concatenate([paired, pushed_rows], axis=0)
        product = dot_nt(left, paired)
        product = jnp.concatenate([product, jnp.zeros((quarter + 16, LANES - quarter), F32)], axis=1)
        schur = product[:quarter]
        low = pltpu.roll(schur[half:], LANES - half, 1)
        send_m[s] = jnp.where(below, low, schur[:half]).astype(BF16)
        send_v[s, 0:1, :] = product[quarter : quarter + 1]
        send_v[s, 1:2, :] = jnp.sum(jnp.where(diag_of, schur, 0.0), axis=0, keepdims=True)

        @pl.when(k == 0)
        def _():
            pl.semaphore_wait(barrier, plane - 1 + inner - 1)
            t_copy.start()

        @pl.when(k < scen_here - 1)
        def _():
            remote(send_m.at[s], recv_m.at[me], 0, (g, s)).start()
            remote(send_v.at[s], recv_v.at[me], 1, (g, s)).start()

        return carry

    lax.fori_loop(0, scen_here, local, 0)

    table[...] = jnp.zeros((8, LANES), F32)
    table[:, 0:split_at] = jnp.broadcast_to(root_ref[...], (8, split_at))
    table[:, split_at:quarter] = bprev_ref[...]
    branch = branch_ref[me]
    anchor = jnp.sum(jnp.where(sub8 == branch, table[...], 0.0), axis=0, keepdims=True)
    mult = jnp.concatenate(
        [mult_ref[pl.ds(me, 1), :], jnp.zeros((1, LANES - quarter), F32)], axis=1
    )
    t_copy.wait_recv()
    far_chance = recv_t[0:1, :]
    far_group = recv_t[1:2, :]
    for i in range(n_clus):
        member = sub8.astype(F32) == far_group[:, i : i + 1]
        chance[other * n_clus + i] = jnp.where(member, far_chance[:, i : i + 1], 0.0)
    mass = chance[0]
    for i in range(1, plane):
        mass = mass + chance[i]
    inv_mass = jnp.where(mass > 0.0, 1.0 / jnp.where(mass > 0.0, mass, 1.0), 0.0)

    recv_m[me] = send_m[me]
    recv_v[me] = send_v[me]
    await_all(recv_m, 0, recv_sem, n_clus - 1)
    await_all(recv_v, 1, recv_sem, n_clus - 1)
    mats = [recv_m[j].astype(F32) for j in range(n_clus)]
    vecs = [recv_v[j] for j in range(n_clus)]
    while len(mats) > 1:
        mats = [mats[i] + mats[i + 1] for i in range(0, len(mats), 2)]
        vecs = [vecs[i] + vecs[i + 1] for i in range(0, len(vecs), 2)]
    mat, vec = mats[0], vecs[0]

    lane_h = iota((half, LANES), 1)
    row_h = iota((half, LANES), 0)
    flipped = jnp.concatenate([mat, jnp.zeros((LANES - half, LANES), F32)], axis=0).T
    flip_a = flipped[:half]
    top = jnp.where(lane_h > row_h, mat, flip_a)
    low = jnp.where(lane_h < row_h, mat, flip_a)
    low = pltpu.roll(low, half, 1)
    bottom = jnp.where(lane_h < half, flipped[half:quarter], low)
    schur = jnp.concatenate([top, bottom], axis=0)
    lane_q = iota((quarter, LANES), 1)
    schur = jnp.where(diag_of, vec[1:2], schur)
    system = jnp.where(diag_of, 1.0 + penalty * schur, penalty * schur)
    system = jnp.where(lane_q < quarter, system, 0.0)
    side = jnp.where(lane1 < quarter, mult - penalty * (vec[0:1] + anchor), 0.0)
    side_rows = jnp.where(sub8 == 0, side, 0.0)
    prices = solve_row(system, side_rows, quarter)
    bid = anchor + (prices - mult) / penalty
    msg[0:1, :] = prices
    msg[1:2, :] = jnp.where(lane1 < quarter, bid, jnp.where(lane1 == quarter, 1.0, 0.0))
    recv_p[my_slot] = msg[...]

    for j in sorted(range(1, plane), key=lambda j: abs(2 * j - plane)):
        slot = lax.rem(my_slot + j, plane)
        remote(msg, recv_p.at[my_slot], 3, plane_device(slot)).start()
    await_all(recv_p, 3, recv_sem, plane - 1)

    def bid_tile(i):
        return jnp.broadcast_to(recv_p[i, 1:2, :], (8, LANES))

    totals = [chance[i] * bid_tile(i) for i in range(plane)]
    while len(totals) > 1:
        totals = [totals[i] + totals[i + 1] for i in range(0, len(totals), 2)]
    mean = totals[0] * inv_mass
    squares = []
    for i in range(plane):
        away = bid_tile(i) - mean
        squares.append(chance[i] * (away * away))
    while len(squares) > 1:
        squares = [squares[i] + squares[i + 1] for i in range(0, len(squares), 2)]
    square = jnp.sum(jnp.where(lane8 < quarter, squares[0], 0.0), axis=0, keepdims=True)
    square = jnp.sum(square, axis=1, keepdims=True)
    stat[...] = jnp.where(
        lane8 < quarter, mean, jnp.where(lane8 == quarter, mass, jnp.where(sub8 == 0, square, 0.0))
    )
    recv_s[my_inner] = stat[...]

    for j in sorted(range(1, inner), key=lambda j: abs(2 * j - inner)):
        slot = lax.rem(my_inner + j, inner)
        remote(stat, recv_s.at[my_inner], 4, line_device(slot)).start()

    def powers(s, carry):
        price = recv_p[my_base + s, 0:1, :][:, :quarter]
        price = jnp.broadcast_to(price, (16, quarter)).astype(BF16)
        step = jnp.dot(price, pt_buf[s], preferred_element_type=F32)
        moved = push_buf[s] + step[0:1]
        stacked = jnp.concatenate(
            [
                jnp.where(row_of, moved[:, :rows], 0.0)[:clus_here],
                jnp.where(row_of, moved[:, rows:], 0.0)[:clus_here],
                jnp.zeros((16 - 2 * clus_here, rows), F32),
            ],
            axis=0,
        ).astype(BF16)
        out = jnp.dot(stacked, jnp.concatenate(tiles_of(s), axis=1), preferred_element_type=F32)
        from_odd = pltpu.roll(out[clus_here : 2 * clus_here, LANES:], LANES + LANES // 2, 1)
        total = out[:clus_here, : 2 * LANES] + from_odd
        power_ref[s] = -total[:, :width]
        return carry

    lax.fori_loop(0, scen_here, powers, 0, unroll=2)
    mine = recv_p[pl.ds(my_base, n_clus), 1, :]
    bid_ref[...] = mine[:, :quarter]
    await_all(send_m, 0, send_sem, n_clus - 1)
    await_all(send_v, 1, send_sem, n_clus - 1)
    t_copy.wait_send()
    await_all(recv_p, 3, send_sem, plane - 1)

    await_all(recv_s, 4, recv_sem, inner - 1)
    parts = [recv_s[j] for j in range(inner)]
    weights = [jnp.broadcast_to(part[:, quarter : quarter + 1], (8, LANES)) for part in parts]
    sums = [part * weight for part, weight in zip(parts, weights)]
    heavy = list(weights)
    while len(sums) > 1:
        sums = [sums[i] + sums[i + 1] for i in range(0, len(sums), 2)]
        heavy = [heavy[i] + heavy[i + 1] for i in range(0, len(heavy), 2)]
    whole = jnp.sum(sums[0], axis=0, keepdims=True)
    whole_mass = jnp.sum(heavy[0], axis=0, keepdims=True)
    node = jnp.where(lane8 < split_at, whole / whole_mass, sums[0] / heavy[0])
    mean_ref[...] = node[:, :quarter]
    target = jnp.zeros((n_clus, LANES), F32)
    for b in range(branch_count):
        target = jnp.where(group_rows == b, node[b : b + 1], target)
    next_ref[...] = mult_ref[...] + penalty * (mine - target)[:, :quarter]
    spread = []
    within = []
    for part, weight in zip(parts, weights):
        away = part - node
        spread.append(weight * (away * away))
        within.append(part[0:1])
    while len(spread) > 1:
        spread = [spread[i] + spread[i + 1] for i in range(0, len(spread), 2)]
        within = [within[i] + within[i + 1] for i in range(0, len(within), 2)]
    both = jnp.sum(jnp.where(lane8 < quarter, spread[0], 0.0), axis=0, keepdims=True)
    both = both + jnp.where(lane1 == quarter + 1, within[0], 0.0)
    gap_ref[...] = jnp.sum(both, axis=1, keepdims=True) / (quarter * whole_mass[:, 0:1])
    await_all(recv_s, 4, send_sem, inner - 1)


def hand_out(*refs):
    count = len(refs) // 2
    sems = refs[-1]
    copies = [
        pltpu.make_async_copy(refs[i], refs[count + i], sems.at[i]) for i in range(count)
    ]
    for copy in copies:
        copy.start()
    for copy in copies:
        copy.wait()


def solution(mesh):
    n_scen, n_clus = mesh.shape["scen"], mesh.shape["clus"]

    def step(
        factors,
        linear,
        arrival,
        departure,
        ev_count,
        prob,
        branch_of,
        multiplier,
        root_prev,
        branch_prev,
    ):
        scen_here, clus_here = factors.shape[:2]
        width = linear.shape[2]
        quarter = multiplier.shape[1]
        split_at = root_prev.shape[0]
        branch_count = branch_prev.shape[0]
        rows = quarter * clus_here
        plane = HALVES * n_clus
        inner = n_scen // HALVES
        tiles = factors.reshape(scen_here, clus_here, 3 * quarter, LANES)
        tiles = tiles.transpose(0, 2, 1, 3).reshape(scen_here, 3 * rows, LANES)
        vmem = pl.BlockSpec(memory_space=pltpu.VMEM)
        dma = pltpu.SemaphoreType.DMA
        shapes = (
            jax.ShapeDtypeStruct((scen_here, clus_here, width), F32),
            jax.ShapeDtypeStruct((scen_here, quarter), F32),
            jax.ShapeDtypeStruct((scen_here, quarter), F32),
            jax.ShapeDtypeStruct((branch_count, quarter), F32),
            jax.ShapeDtypeStruct((1, 1), F32),
        )
        results = pl.pallas_call(
            functools.partial(
                kernel, n_scen, n_clus, clus_here, quarter, split_at, branch_count
            ),
            out_shape=tuple(pltpu.VMEM(shape.shape, shape.dtype) for shape in shapes),
            in_specs=[pl.BlockSpec(memory_space=pl.ANY)] * 10,
            out_specs=(vmem,) * 5,
            scratch_shapes=[
                pltpu.VMEM((scen_here, 3 * rows, LANES), BF16),
                pltpu.VMEM(linear.shape, F32),
                pltpu.SMEM((clus_here, scen_here), jnp.int32),
                pltpu.SMEM((clus_here, scen_here), jnp.int32),
                pltpu.SMEM((clus_here,), jnp.int32),
                pltpu.SMEM((scen_here,), F32),
                pltpu.SMEM((scen_here,), jnp.int32),
                pltpu.VMEM(multiplier.shape, F32),
                pltpu.VMEM((1, split_at), F32),
                pltpu.VMEM(branch_prev.shape, F32),
                pltpu.VMEM((scen_here, quarter, 2 * rows), BF16),
                pltpu.VMEM((scen_here, 1, 2 * rows), F32),
                pltpu.VMEM((quarter, 2 * LANES), BF16),
                pltpu.VMEM((quarter, 2 * LANES), BF16),
                pltpu.VMEM((8, LANES), F32),
                pltpu.VMEM((plane, 8, LANES), F32),
                pltpu.VMEM((n_clus, quarter // 2, LANES), BF16),
                pltpu.VMEM((n_clus, 2, LANES), F32),
                pltpu.VMEM((n_clus, quarter // 2, LANES), BF16),
                pltpu.VMEM((n_clus, 2, LANES), F32),
                pltpu.VMEM((2, LANES), F32),
                pltpu.VMEM((2, LANES), F32),
                pltpu.VMEM((2, LANES), F32),
                pltpu.VMEM((plane, 2, LANES), F32),
                pltpu.VMEM((8, LANES), F32),
                pltpu.VMEM((inner, 8, LANES), F32),
                dma((9,)),
                dma((scen_here,)),
                dma((5,)),
                dma((5,)),
            ],
            compiler_params=pltpu.CompilerParams(collective_id=0, has_side_effects=True),
        )(
            tiles,
            linear,
            arrival.T,
            departure.T,
            ev_count,
            prob,
            branch_of,
            multiplier,
            root_prev[None, :],
            branch_prev,
        )
        power, bid, following, mean, gap = pl.pallas_call(
            hand_out,
            out_shape=shapes,
            in_specs=[vmem] * 5,
            out_specs=(pl.BlockSpec(memory_space=pl.ANY),) * 5,
            scratch_shapes=[dma((5,))],
        )(*[pltpu.with_memory_space_constraint(result, pltpu.VMEM) for result in results])
        return (power, bid, following, mean, gap.reshape(()))

    return jax.shard_map(
        step,
        mesh=mesh,
        in_specs=(
            P("scen", "clus", None),
            P("scen", "clus", None),
            P("scen", "clus"),
            P("scen", "clus"),
            P("clus"),
            P("scen"),
            P("scen"),
            P("scen", None),
            P(),
            P(),
        ),
        out_specs=(P("scen", "clus", None), P("scen", None), P("scen", None), P(), P()),
        check_vma=False,
    )
```
